512 devices in a mesh: rep: 8 (over z_hi, core), fsdp: 64 (over y, x, z_lo).
Axes of the slice: x: 4, y: 8, z: 8 (z_hi: 4, z_lo: 2; z = z_hi * 2 + z_lo), core: 2. Of those that a mesh axis runs over, the one named last changes fastest.
Arguments:
- acts: bfloat16 [8, 8192, 8192], P('rep', 'fsdp'), may hold values from -16 to 16
- value_cots: bfloat16 [8, 8192, 512], P('rep', 'fsdp'), may hold values from -0.059814453 to 0.059814453
- inner_weights: float32 [8, 8192, 512], P('rep', 'fsdp'), may hold values from -0.0625 to 0.0625
- first_moment: float32 [8, 8192, 512], P('rep', 'fsdp'), may hold values from -1.8 to 1.8
- second_moment: float32 [8, 8192, 512], P('rep', 'fsdp'), may hold values from 0.01 to 1
- anchor: float32 [8192, 512], P('fsdp'), may hold values from -0.0625 to 0.0625
- outer_momentum: float32 [8192, 512], P('fsdp'), may hold values from -0.06 to 0.06
Outputs:
- first_next: float32 [8, 8192, 512], P('rep', 'fsdp')
- values_next: bfloat16 [8, 8192, 512], P('rep', 'fsdp')
The draws below stay inside these ranges and needn't reach their ends.
All inputs are finite; a program needn't handle non-finite values.
Results may differ from the reference program's by a relative error of at most 0.0049.
Values may be sent and summed in bfloat16 or wider, within the bound.
A program may use at most 64 MiB of HBM per device.

```python
import math
from functools import partial
import jax
import jax.numpy as jnp
from jax import lax

D = 8192
C = 512
TOKENS = 8192
N_REP = 8


def strengthened(result, rng, source, target, parts, factor):
    def block_of(dim):
        return (jnp.arange(result.shape[dim]) // (result.shape[dim] // parts)).reshape((-1,) + (1,) * (result.ndim - 1 - dim))

    first = jax.random.permutation(rng, parts)[block_of(target)]
    far = (block_of(target) + parts // 2) % parts
    return jnp.where((block_of(source) == first) | (block_of(source) == far), factor * result, result)


def block_levels(key, dims, pieces, least, top_value):
    def one(axis_at, shards_of):
        steps = jax.random.uniform(jax.random.fold_in(jax.random.fold_in(key, 6), axis_at), (shards_of,), jnp.float32, least / len(pieces), top_value / len(pieces))
        return jnp.repeat(jnp.exp(steps), dims[axis_at] // shards_of).reshape((-1,) + (1,) * (len(dims) - axis_at - 1))

    level = one(*pieces[0])
    for cut in pieces[1:]:
        level = level * one(*cut)
    return level


def normal_values(own_key, dims, scale, limit, split=(), kind=jnp.bfloat16):
    level = block_levels(own_key, dims, split, -0.22, 0.18) if split else 1.0
    drawn = jax.random.normal(own_key, dims, jnp.float32) * scale * level
    return jnp.minimum(jnp.maximum(drawn, -limit), limit).astype(kind)


def gaussian_with(rng, shape, deviation, bound, cuts, heavy, held_as=jnp.bfloat16):
    array = deviation * jax.random.normal(rng, shape, jnp.float32)
    if cuts:
        array = array * block_levels(rng, shape, cuts, -0.22, 0.18)
    return jnp.clip(strengthened(array, jax.random.fold_in(rng, 3), *heavy), -bound, bound).astype(held_as)


def setup_inputs(seed: int = 0) -> dict:
    key_of = jax.random.split(jax.random.key(seed), 8)
    acts = gaussian_with(key_of[0], (N_REP, TOKENS, D), 1.0, 16.0, ((0, 8), (1, 64)), (1, 2, 64, 4.0))
    value_cots = normal_values(key_of[1], (N_REP, TOKENS, C), 0.01, 0.059814453, ((0, 8), (1, 64)))
    inner_weights = normal_values(key_of[2], (N_REP, D, C), D ** -0.5, 0.0625, ((0, 8), (1, 64)), jnp.float32)
    first_moment = normal_values(key_of[3], (N_REP, D, C), 0.3, 1.8, ((0, 8), (1, 64)), jnp.float32)
    second_moment = jnp.clip(jnp.exp(math.log(1.0) - 4.6051702 * jax.random.uniform(key_of[4], (N_REP, D, C), jnp.float32) ** block_levels(key_of[4], (N_REP, D, C), ((0, 8), (1, 64)), -0.2, 0.2)), 0.01, 1.0)
    anchor = normal_values(key_of[5], (D, C), D ** -0.5, 0.0625, ((0, 64),), jnp.float32)
    outer_momentum = normal_values(key_of[6], (D, C), 0.01, 0.06, ((0, 64),), jnp.float32)
    return {"acts": acts, "value_cots": value_cots, "inner_weights": inner_weights, "first_moment": first_moment, "second_moment": second_moment, "anchor": anchor, "outer_momentum": outer_momentum}


decay_first = 0.9
decay_second = 0.95
inner_rate = 0.006
epsilon = 1e-08
outer_rate = 0.7
outer_decay = 0.9

def replica_step(anchor, packed):
    tokens, cots, weights, first, second = packed
    gradient = lax.dot_general(tokens, cots, (((0,), (0,)), ((), ())), preferred_element_type=jnp.float32)
    first_next = decay_first * first + (1.0 - decay_first) * gradient
    second_next = decay_second * second + (1.0 - decay_second) * gradient * gradient
    stepped = weights - inner_rate * first_next / (jnp.sqrt(second_next) + epsilon)
    return (first_next, anchor - stepped)

def forward_rows(weights_next, tokens):
    return jnp.dot(tokens, weights_next, preferred_element_type=jnp.float32).astype(jnp.bfloat16)

def reference(acts, value_cots, inner_weights, first_moment, second_moment, anchor, outer_momentum):
    firsts, drifts = lax.map(partial(replica_step, anchor), (acts, value_cots, inner_weights, first_moment, second_moment))
    drift = lax.optimization_barrier(jnp.sum(drifts, axis=0)) / N_REP
    velocity = outer_decay * outer_momentum + drift
    weights_next = (anchor - outer_rate * (drift + outer_decay * velocity)).astype(jnp.bfloat16)
    values_next = lax.map(partial(forward_rows, weights_next), acts)
    return (firsts, values_next)
```

```python
import jax
import jax.numpy as jnp
from jax import lax
from jax.experimental import pallas as pl
from jax.experimental.pallas import tpu as pltpu
from jax.sharding import PartitionSpec as P

decay_first = 0.9
decay_second = 0.95
inner_rate = 0.006
epsilon = 1e-08
outer_rate = 0.7
outer_decay = 0.9

MESH = pl.DeviceIdType.MESH
F32 = jnp.float32
BF16 = jnp.bfloat16

Y = 8
J = 8
Z = 4
B = 128
C = 512
OFFSETS = (4, 3, 5, 2, 6, 1, 7, 0)
SLOT = {off: k for k, off in enumerate(OFFSETS)}
OWN = SLOT[0]


def step_kernel(
    acts, cots, inner, first, second, anchor, momentum, first_out, values_out,
    a_buf, c_buf, state, first_buf, go_up, go_down, from_down, from_up,
    drift_buf, drift_pair, pair_sum, z_buf, w_buf, v_send, v_recv,
    state_sem, cots_s, cots_r, acts_s, acts_r, up_s, up_r, down_s, down_r,
    pair_s, pair_r, z_s, z_r, wz_s, wz_r, wy_s, wy_r, wc_s, wc_r, v_s, v_r, out_sem,
):
    f = lax.axis_index("fsdp")
    r = lax.axis_index("rep")
    y, j = lax.div(f, J), lax.rem(f, J)
    zh, core = lax.div(r, 2), lax.rem(r, 2)

    def in_plane(d):
        return {"fsdp": y * J + lax.rem(j + d, J)}

    def along_y(t):
        return {"fsdp": lax.rem(y + t, Y) * J + j}

    def along_z(q):
        return {"rep": lax.rem(zh + q, Z) * 2 + core}

    sibling = {"rep": zh * 2 + 1 - core}

    def remote(src, dst, send, recv, device):
        return pltpu.make_async_remote_copy(
            src_ref=src, dst_ref=dst, send_sem=send, recv_sem=recv, device_id=device, device_id_type=MESH
        )

    def rows(start, size):
        return pl.ds(pl.multiple_of(start, size), size)

    loads = [
        pltpu.make_async_copy(ref, state.at[i], state_sem.at[i])
        for i, ref in enumerate((inner, first, second, anchor, momentum))
    ]
    for load in loads:
        load.start()
    own_cots = pltpu.make_async_copy(cots, c_buf.at[rows(j * B, B)], cots_r.at[0])
    own_cots.start()

    def acts_block(k, target):
        return acts.at[:, rows((lax.rem(y + OFFSETS[k], Y) * J + target) * B, B)]

    own_acts = []
    for k in range(Y):
        copy = pltpu.make_async_copy(
            acts_block(k, j), a_buf.at[rows(j * B, B), pl.ds(k * B, B)], acts_r.at[k, 0]
        )
        copy.start()
        own_acts.append(copy)

    barrier = pltpu.get_barrier_semaphore()
    for d in range(1, J):
        pl.semaphore_signal(barrier, inc=1, device_id=in_plane(d), device_id_type=MESH)
    for t in range(1, Y):
        pl.semaphore_signal(barrier, inc=1, device_id=along_y(t), device_id_type=MESH)
    for q in range(1, Z):
        pl.semaphore_signal(barrier, inc=1, device_id=along_z(q), device_id_type=MESH)
    pl.semaphore_signal(barrier, inc=1, device_id=sibling, device_id_type=MESH)
    pl.semaphore_wait(barrier, J - 1 + Y - 1 + Z - 1 + 1)

    def cots_copy(d):
        return remote(cots, c_buf.at[rows(j * B, B)], cots_s.at[d], cots_r.at[d], in_plane(d))

    def cots_arrival(d):
        return remote(cots, c_buf.at[rows(lax.rem(j + J - d, J) * B, B)], cots_s.at[d], cots_r.at[d], in_plane(d))

    def acts_copy(k, d):
        return remote(
            acts_block(k, lax.rem(j + d, J)), a_buf.at[rows(j * B, B), pl.ds(k * B, B)],
            acts_s.at[k, d], acts_r.at[k, d], in_plane(d),
        )

    def acts_arrival(k, d):
        return remote(
            acts_block(k, j), a_buf.at[rows(lax.rem(j + J - d, J) * B, B), pl.ds(k * B, B)],
            acts_s.at[k, d], acts_r.at[k, d], in_plane(d),
        )

    def each(low, high, body):
        def step(i, carry):
            body(i)
            return carry

        lax.fori_loop(low, high, step, 0)

    each(1, J, lambda d: cots_copy(d).start())
    for k in range(Y):
        each(1, J, lambda d, k=k: acts_copy(k, d).start())

    own_cots.wait()
    each(1, J, lambda d: cots_arrival(d).wait_recv())

    def partial_gradient(k):
        own_acts[k].wait()
        each(1, J, lambda d: acts_arrival(k, d).wait_recv())
        return lax.dot_general(
            a_buf[:, pl.ds(k * B, B)], c_buf[...], (((0,), (0,)), ((), ())), preferred_element_type=F32
        )

    half = C // 2
    low, high = pl.ds(0, half), pl.ds(half, half)
    part = partial_gradient(SLOT[4])
    go_up[0, :, low] = part[:, :half]
    go_down[0, :, high] = part[:, half:]

    def up_copy(i):
        cols = low if i == 0 else pl.ds(0, C)
        return remote(go_up.at[i, :, cols], from_down.at[i, :, cols], up_s.at[i], up_r.at[i], along_y(1))

    def down_copy(i):
        cols = high if i == 0 else pl.ds(0, C)
        return remote(go_down.at[i, :, cols], from_up.at[i, :, cols], down_s.at[i], down_r.at[i], along_y(Y - 1))

    ups = [up_copy(i) for i in range(4)]
    downs = [down_copy(i) for i in range(4)]
    ups[0].start()
    downs[0].start()
    for i in range(1, 4):
        part = partial_gradient(SLOT[4 - i])
        ups[i - 1].wait_recv()
        if i == 1:
            go_up[1, :, low] = part[:, :half] + from_down[0, :, low]
            go_up[1, :, high] = part[:, half:]
        else:
            go_up[i] = part + from_down[i - 1]
        ups[i].start()
        part = partial_gradient(SLOT[4 + i])
        downs[i - 1].wait_recv()
        if i == 1:
            go_down[1, :, low] = part[:, :half]
            go_down[1, :, high] = part[:, half:] + from_up[0, :, high]
        else:
            go_down[i] = part + from_up[i - 1]
        downs[i].start()
    part = partial_gradient(OWN)
    ups[3].wait_recv()
    downs[3].wait_recv()
    gradient = part + from_down[3] + from_up[3]

    for load in loads:
        load.wait()
    first_next = decay_first * state[1] + (1.0 - decay_first) * gradient
    first_buf[...] = first_next
    store_first = pltpu.make_async_copy(first_buf, first_out, out_sem)
    store_first.start()
    second_next = decay_second * state[2] + (1.0 - decay_second) * gradient * gradient
    stepped = state[0] - inner_rate * first_next / (jnp.sqrt(second_next) + epsilon)
    drift_buf[...] = state[3] - stepped

    H = B // 2
    Q = H // Z
    pair = remote(drift_buf.at[rows((1 - core) * H, H)], drift_pair, pair_s, pair_r, sibling)
    pair.start()
    pair.wait_recv()
    pair_sum[...] = drift_buf[rows(core * H, H), :] + drift_pair[...]

    def z_copy(q):
        return remote(
            pair_sum.at[rows(lax.rem(zh + q, Z) * Q, Q)], z_buf.at[q], z_s.at[q], z_r.at[q], along_z(q)
        )

    zs = [z_copy(q) for q in range(1, Z)]
    for copy in zs:
        copy.start()
    total = pair_sum[rows(zh * Q, Q), :]
    for q in range(1, Z):
        zs[q - 1].wait_recv()
        total = total + z_buf[q]
    mine = core * H + zh * Q
    anchor_rows = state[3, rows(mine, Q), :]
    momentum_rows = state[4, rows(mine, Q), :]
    average = total / (2 * Z)
    velocity = outer_decay * momentum_rows + average
    weights = (anchor_rows - outer_rate * (average + outer_decay * velocity)).astype(BF16)
    w_buf[rows(OWN * B + mine, Q), :] = weights

    def wz_copy(q):
        here = w_buf.at[rows(OWN * B + mine, Q)]
        return remote(here, here, wz_s.at[q], wz_r.at[q], along_z(q))

    def wz_arrival(q):
        there = w_buf.at[rows(OWN * B + core * H + lax.rem(zh + Z - q, Z) * Q, Q)]
        return remote(there, there, wz_s.at[q], wz_r.at[q], along_z(q))

    wzs = [wz_copy(q) for q in range(1, Z)]
    for copy in wzs:
        copy.start()
    for q in range(1, Z):
        wz_arrival(q).wait_recv()

    def w_half(t, side):
        return w_buf.at[rows(SLOT[(Y - t) % Y] * B + side * H, H)]

    near_first = (4, 3, 5, 2, 6, 1, 7)
    wys = {t: remote(w_half(0, core), w_half(t, core), wy_s.at[t], wy_r.at[t], along_y(t)) for t in near_first}
    for t in near_first:
        wys[t].start()
    forwards = {t: remote(w_half(t, core), w_half(t, core), wc_s.at[t], wc_r.at[t], sibling) for t in range(Y)}
    forwards[0].start()
    for t in reversed(near_first):
        wys[t].wait_recv()
        forwards[t].start()
    for t in range(Y):
        remote(w_half(t, 1 - core), w_half(t, 1 - core), wc_s.at[t], wc_r.at[t], sibling).wait_recv()

    def values_of(target):
        return jnp.dot(a_buf[rows(target * B, B), :], w_buf[...], preferred_element_type=F32)

    def v_copy(d):
        return remote(v_send.at[d], v_recv.at[d], v_s.at[d], v_r.at[d], in_plane(d))

    def send_values(d):
        v_send[d] = values_of(lax.rem(j + d, J)).astype(BF16)
        v_copy(d).start()

    each(1, J, send_values)
    total = values_of(j)
    for d in range(1, J):
        v_copy(d).wait_recv()
        total = total + v_recv[d].astype(F32)
    values_out[...] = total.astype(BF16)

    store_first.wait()
    each(1, J, lambda d: cots_copy(d).wait_send())
    for k in range(Y):
        each(1, J, lambda d, k=k: acts_copy(k, d).wait_send())
    for i in range(4):
        ups[i].wait_send()
        downs[i].wait_send()
    pair.wait_send()
    for copy in zs + wzs:
        copy.wait_send()
    for t in near_first:
        wys[t].wait_send()
    for t in range(Y):
        forwards[t].wait_send()
    each(1, J, lambda d: v_copy(d).wait_send())


def on_device(acts, value_cots, inner_weights, first_moment, second_moment, anchor, outer_momentum):
    dma = pltpu.SemaphoreType.DMA
    vmem = pltpu.VMEM
    first_next, values = pl.pallas_call(
        step_kernel,
        name="diloco_step",
        out_shape=(jax.ShapeDtypeStruct((B, C), F32), jax.ShapeDtypeStruct((B, C), BF16)),
        in_specs=[pl.BlockSpec(memory_space=pl.ANY)] * 7,
        out_specs=(pl.BlockSpec(memory_space=pl.ANY), pl.BlockSpec(memory_space=pltpu.VMEM)),
        scratch_shapes=[
            vmem((J * B, Y * B), BF16),
            vmem((J * B, C), BF16),
            vmem((5, B, C), F32),
            vmem((B, C), F32),
            vmem((4, B, C), F32),
            vmem((4, B, C), F32),
            vmem((4, B, C), F32),
            vmem((4, B, C), F32),
            vmem((B, C), F32),
            vmem((B // 2, C), F32),
            vmem((B // 2, C), F32),
            vmem((Z, B // 2 // Z, C), F32),
            vmem((Y * B, C), BF16),
            vmem((J, B, C), BF16),
            vmem((J, B, C), BF16),
            dma((5,)),
            dma((J,)), dma((J,)),
            dma((Y, J)), dma((Y, J)),
            dma((4,)), dma((4,)), dma((4,)), dma((4,)),
            dma(()), dma(()),
            dma((Z,)), dma((Z,)),
            dma((Z,)), dma((Z,)),
            dma((Y,)), dma((Y,)),
            dma((Y,)), dma((Y,)),
            dma((J,)), dma((J,)),
            dma(()),
        ],
        compiler_params=pltpu.CompilerParams(
            collective_id=0, has_side_effects=True, vmem_limit_bytes=40 * 1024 * 1024
        ),
    )(acts[0], value_cots[0], inner_weights[0], first_moment[0], second_moment[0], anchor, outer_momentum)
    return first_next[None], values[None]


def solution(mesh):
    placed = (
        P("rep", "fsdp", None),
        P("rep", "fsdp", None),
        P("rep", "fsdp", None),
        P("rep", "fsdp", None),
        P("rep", "fsdp", None),
        P("fsdp", None),
        P("fsdp", None),
    )
    return jax.shard_map(
        on_device,
        mesh=mesh,
        in_specs=placed,
        out_specs=(P("rep", "fsdp", None), P("rep", "fsdp", None)),
        check_vma=False,
    )
```

```python
import jax
import jax.numpy as jnp
from jax import lax
from jax.experimental import pallas as pl
from jax.experimental.pallas import tpu as pltpu
from jax.sharding import PartitionSpec as P

decay_first = 0.9
decay_second = 0.95
inner_rate = 0.006
epsilon = 1e-08
outer_rate = 0.7
outer_decay = 0.9

MESH = pl.DeviceIdType.MESH
F32 = jnp.float32
BF16 = jnp.bfloat16

Y = 8
J = 8
Z = 4
B = 128
C = 512
OFFSETS = (4, 3, 5, 2, 6, 1, 7, 0)
SLOT = {off: k for k, off in enumerate(OFFSETS)}
OWN = SLOT[0]


def step_kernel(
    acts, cots, inner, first, second, anchor, momentum, first_out, values_out,
    a_buf, c_buf, state, first_buf, go_up, go_down, from_down, from_up,
    drift_buf, drift_pair, pair_sum, z_buf, w_buf, v_send, v_recv, v_out,
    state_sem, cots_own, cots_s, cots_r, acts_own, acts_s, acts_r, up_s, up_r, down_s, down_r,
    pair_s, pair_r, z_s, z_r, wz_s, wz_r, wy_s, wy_r, wc_s, wc_r, v_s, v_r, first_sem, values_sem,
):
    f = lax.axis_index("fsdp")
    r = lax.axis_index("rep")
    y, j = lax.div(f, J), lax.rem(f, J)
    zh, core = lax.div(r, 2), lax.rem(r, 2)
    plane_peer = [lax.rem(j + d, J) for d in range(J)]
    in_plane = [{"fsdp": y * J + plane_peer[d]} for d in range(J)]
    along_y = [{"fsdp": lax.rem(y + t, Y) * J + j} for t in range(Y)]
    along_z = [{"rep": lax.rem(zh + q, Z) * 2 + core} for q in range(Z)]
    sibling = {"rep": zh * 2 + 1 - core}

    def remote(src, dst, send, recv, device):
        return pltpu.make_async_remote_copy(
            src_ref=src, dst_ref=dst, send_sem=send, recv_sem=recv, device_id=device, device_id_type=MESH
        )

    def rows(start, size):
        return pl.ds(pl.multiple_of(start, size), size)

    barrier = pltpu.get_barrier_semaphore()
    for device in in_plane[1:] + along_y[1:] + along_z[1:] + [sibling]:
        pl.semaphore_signal(barrier, inc=1, device_id=device, device_id_type=MESH)

    own_cots = pltpu.make_async_copy(cots, c_buf.at[rows(j * B, B)], cots_own)
    own_cots.start()

    def acts_block(k, target):
        return acts.at[:, rows((lax.rem(y + OFFSETS[k], Y) * J + target) * B, B)]

    own_acts = [
        pltpu.make_async_copy(acts_block(k, j), a_buf.at[rows(j * B, B), pl.ds(k * B, B)], acts_own.at[k])
        for k in range(Y)
    ]
    for copy in own_acts:
        copy.start()
    loads = [
        pltpu.make_async_copy(ref, state.at[i], state_sem.at[i])
        for i, ref in enumerate((inner, first, second, anchor, momentum))
    ]
    for load in loads:
        load.start()
    pl.semaphore_wait(barrier, J - 1 + Y - 1 + Z - 1 + 1)

    for d in range(1, J):
        remote(cots, c_buf.at[rows(j * B, B)], cots_s, cots_r, in_plane[d]).start()
    for k in range(Y):
        for d in range(1, J):
            remote(
                acts_block(k, plane_peer[d]), a_buf.at[rows(j * B, B), pl.ds(k * B, B)],
                acts_s.at[k], acts_r.at[k], in_plane[d],
            ).start()

    others = pl.ds(0, (J - 1) * B)
    all_cots = remote(c_buf.at[others], c_buf.at[others], cots_s, cots_r, in_plane[1])

    def acts_arrivals(k):
        block = a_buf.at[others, pl.ds(k * B, B)]
        return remote(block, block, acts_s.at[k], acts_r.at[k], in_plane[1])

    own_cots.wait()
    all_cots.wait_recv()

    def partial_gradient(k):
        own_acts[k].wait()
        acts_arrivals(k).wait_recv()
        return lax.dot_general(
            a_buf[:, pl.ds(k * B, B)], c_buf[...], (((0,), (0,)), ((), ())), preferred_element_type=F32
        )

    half = C // 2
    halves = (pl.ds(0, half), pl.ds(half, half))
    low, high = halves
    part = partial_gradient(SLOT[4])
    go_up[0, :, low] = part[:, :half]
    go_down[0, :, high] = part[:, half:]

    def up_copy(i):
        cols = low if i == 0 else pl.ds(0, C)
        return remote(go_up.at[i, :, cols], from_down.at[i, :, cols], up_s.at[i], up_r.at[i], along_y[1])

    def down_copy(i):
        cols = high if i == 0 else pl.ds(0, C)
        return remote(go_down.at[i, :, cols], from_up.at[i, :, cols], down_s.at[i], down_r.at[i], along_y[Y - 1])

    ups = [up_copy(i) for i in range(4)]
    downs = [down_copy(i) for i in range(4)]
    ups[0].start()
    downs[0].start()
    for i in range(1, 4):
        part = partial_gradient(SLOT[4 - i])
        ups[i - 1].wait_recv()
        if i == 1:
            go_up[1, :, low] = part[:, :half] + from_down[0, :, low]
            go_up[1, :, high] = part[:, half:]
        else:
            go_up[i] = part + from_down[i - 1]
        ups[i].start()
        part = partial_gradient(SLOT[4 + i])
        downs[i - 1].wait_recv()
        if i == 1:
            go_down[1, :, low] = part[:, :half]
            go_down[1, :, high] = part[:, half:] + from_up[0, :, high]
        else:
            go_down[i] = part + from_up[i - 1]
        downs[i].start()
    drift_buf[...] = partial_gradient(OWN)
    for load in loads:
        load.wait()
    ups[3].wait_recv()
    downs[3].wait_recv()

    H = B // 2
    Q = H // Z
    mine = core * H + zh * Q
    sent = []

    def inner_step(s):
        cols = halves[s]
        gradient = drift_buf[:, cols] + from_down[3, :, cols] + from_up[3, :, cols]
        first_next = decay_first * state[1, :, cols] + (1.0 - decay_first) * gradient
        first_buf[:, cols] = first_next
        second_next = decay_second * state[2, :, cols] + (1.0 - decay_second) * gradient * gradient
        stepped = state[0, :, cols] - inner_rate * first_next / (jnp.sqrt(second_next) + epsilon)
        drift_buf[:, cols] = state[3, :, cols] - stepped
        pairs[s].start()

    pairs = [
        remote(
            drift_buf.at[rows((1 - core) * H, H), halves[s]], drift_pair.at[:, halves[s]],
            pair_s.at[s], pair_r.at[s], sibling,
        )
        for s in range(2)
    ]
    zs = [
        [
            remote(
                pair_sum.at[rows(lax.rem(zh + q, Z) * Q, Q), halves[s]], z_buf.at[q, :, halves[s]],
                z_s.at[s, q], z_r.at[s, q], along_z[q],
            )
            for q in range(1, Z)
        ]
        for s in range(2)
    ]

    def sum_cores(s):
        cols = halves[s]
        pairs[s].wait_recv()
        pair_sum[:, cols] = drift_buf[rows(core * H, H), cols] + drift_pair[:, cols]
        for copy in zs[s]:
            copy.start()

    def wz_copy(s, q):
        here = w_buf.at[rows(OWN * B + mine, Q), halves[s]]
        return remote(here, here, wz_s.at[s, q], wz_r.at[s, q], along_z[q])

    def wz_arrival(s, q):
        there = w_buf.at[rows(OWN * B + core * H + lax.rem(zh + Z - q, Z) * Q, Q), halves[s]]
        return remote(there, there, wz_s.at[s, q], wz_r.at[s, q], along_z[q])

    wzs = [[wz_copy(s, q) for q in range(1, Z)] for s in range(2)]

    def outer_step(s):
        cols = halves[s]
        total = pair_sum[rows(zh * Q, Q), cols]
        for q in range(1, Z):
            zs[s][q - 1].wait_recv()
            total = total + z_buf[q, :, cols]
        average = total / (2 * Z)
        velocity = outer_decay * state[4, rows(mine, Q), cols] + average
        weights = state[3, rows(mine, Q), cols] - outer_rate * (average + outer_decay * velocity)
        w_buf[rows(OWN * B + mine, Q), cols] = weights.astype(BF16)
        for copy in wzs[s]:
            copy.start()

    def w_half(s, t, side):
        return w_buf.at[rows(SLOT[(Y - t) % Y] * B + side * H, H), halves[s]]

    near_first = (4, 3, 5, 2, 6, 1, 7)
    wys = [
        {t: remote(w_half(s, 0, core), w_half(s, t, core), wy_s.at[s, t], wy_r.at[s, t], along_y[t]) for t in near_first}
        for s in range(2)
    ]
    forwards = [
        [remote(w_half(s, t, core), w_half(s, t, core), wc_s.at[s, t], wc_r.at[s, t], sibling) for t in range(Y)]
        for s in range(2)
    ]

    def spread(s):
        for q in range(1, Z):
            wz_arrival(s, q).wait_recv()
        for t in near_first:
            wys[s][t].start()
        forwards[s][0].start()

    def to_sibling(s):
        for t in reversed(near_first):
            wys[s][t].wait_recv()
            forwards[s][t].start()

    def values_of(s, d):
        return jnp.dot(a_buf[rows(plane_peer[d] * B, B), :], w_buf[:, halves[s]], preferred_element_type=F32)

    vs = [
        [remote(v_send.at[s, d], v_recv.at[s, d], v_s.at[s, d], v_r.at[s, d], in_plane[d]) for d in range(1, J)]
        for s in range(2)
    ]

    def send_values(s):
        for t in range(Y):
            there = w_half(s, t, 1 - core)
            remote(there, there, wc_s.at[s, t], wc_r.at[s, t], sibling).wait_recv()
        for d in range(1, J):
            v_send[s, d] = values_of(s, d).astype(BF16)
            vs[s][d - 1].start()

    stores = [
        pltpu.make_async_copy(v_out.at[:, halves[s]], values_out.at[:, halves[s]], values_sem.at[s]) for s in range(2)
    ]

    def sum_values(s):
        total = values_of(s, 0)
        for d in range(1, J):
            vs[s][d - 1].wait_recv()
            total = total + v_recv[s, d].astype(F32)
        v_out[:, halves[s]] = total.astype(BF16)
        stores[s].start()

    inner_step(0)
    inner_step(1)
    store_first = pltpu.make_async_copy(first_buf, first_out, first_sem)
    store_first.start()
    sum_cores(0)
    sum_cores(1)
    outer_step(0)
    outer_step(1)
    spread(0)
    spread(1)
    to_sibling(0)
    send_values(0)
    to_sibling(1)
    send_values(1)
    sum_values(0)
    sum_values(1)

    all_cots.wait_send()
    for k in range(Y):
        acts_arrivals(k).wait_send()
    for copy in ups + downs + pairs:
        copy.wait_send()
    for s in range(2):
        for copy in zs[s] + wzs[s] + list(wys[s].values()) + forwards[s] + vs[s]:
            copy.wait_send()
    store_first.wait()
    for store in stores:
        store.wait()


def on_device(acts, value_cots, inner_weights, first_moment, second_moment, anchor, outer_momentum):
    dma = pltpu.SemaphoreType.DMA
    vmem = pltpu.VMEM
    first_next, values = pl.pallas_call(
        step_kernel,
        name="diloco_step",
        out_shape=(jax.ShapeDtypeStruct((B, C), F32), jax.ShapeDtypeStruct((B, C), BF16)),
        in_specs=[pl.BlockSpec(memory_space=pl.ANY)] * 7,
        out_specs=(pl.BlockSpec(memory_space=pl.ANY), pl.BlockSpec(memory_space=pl.ANY)),
        scratch_shapes=[
            vmem((J * B, Y * B), BF16),
            vmem((J * B, C), BF16),
            vmem((5, B, C), F32),
            vmem((B, C), F32),
            vmem((4, B, C), F32),
            vmem((4, B, C), F32),
            vmem((4, B, C), F32),
            vmem((4, B, C), F32),
            vmem((B, C), F32),
            vmem((B // 2, C), F32),
            vmem((B // 2, C), F32),
            vmem((Z, B // 2 // Z, C), F32),
            vmem((Y * B, C), BF16),
            vmem((2, J, B, C // 2), BF16),
            vmem((2, J, B, C // 2), BF16),
            vmem((B, C), BF16),
            dma((5,)),
            dma(()), dma(()), dma(()),
            dma((Y,)), dma((Y,)), dma((Y,)),
            dma((4,)), dma((4,)), dma((4,)), dma((4,)),
            dma((2,)), dma((2,)),
            dma((2, Z)), dma((2, Z)),
            dma((2, Z)), dma((2, Z)),
            dma((2, Y)), dma((2, Y)),
            dma((2, Y)), dma((2, Y)),
            dma((2, J)), dma((2, J)),
            dma(()), dma((2,)),
        ],
        compiler_params=pltpu.CompilerParams(
            collective_id=0, has_side_effects=True, vmem_limit_bytes=62 * 1024 * 1024
        ),
    )(acts[0], value_cots[0], inner_weights[0], first_moment[0], second_moment[0], anchor, outer_momentum)
    return first_next[None], values[None]


def solution(mesh):
    placed = (
        P("rep", "fsdp", None),
        P("rep", "fsdp", None),
        P("rep", "fsdp", None),
        P("rep", "fsdp", None),
        P("rep", "fsdp", None),
        P("fsdp", None),
        P("fsdp", None),
    )
    return jax.shard_map(
        on_device,
        mesh=mesh,
        in_specs=placed,
        out_specs=(P("rep", "fsdp", None), P("rep", "fsdp", None)),
        check_vma=False,
    )
```

```python
import jax
import jax.numpy as jnp
from jax import lax
from jax.experimental import pallas as pl
from jax.experimental.pallas import tpu as pltpu
from jax.sharding import PartitionSpec as P

decay_first = 0.9
decay_second = 0.95
inner_rate = 0.006
epsilon = 1e-08
outer_rate = 0.7
outer_decay = 0.9

MESH = pl.DeviceIdType.MESH
F32 = jnp.float32
BF16 = jnp.bfloat16

Y = 8
J = 8
Z = 4
B = 128
C = 512
OFFSETS = (4, 3, 5, 2, 6, 1, 7, 0)
SLOT = {off: k for k, off in enumerate(OFFSETS)}
OWN = SLOT[0]
CHAIN = 2
SLICES = 4


def step_kernel(
    acts, cots, inner, first, second, anchor, momentum, first_out, values_out,
    a_buf, c_buf, state, first_buf, go_up, go_down, from_down, from_up,
    drift_buf, drift_pair, z_buf, w_buf, v_send, v_recv, v_out,
    state_sem, cots_own, cots_s, cots_r, acts_own, acts_s, acts_r, up_s, up_r, down_s, down_r,
    pair_s, pair_r, z_s, z_r, wy_s, wy_r, wc_s, wc_r, v_s, v_r, first_sem, values_sem,
):
    f = lax.axis_index("fsdp")
    r = lax.axis_index("rep")
    y, j = lax.div(f, J), lax.rem(f, J)
    zh, core = lax.div(r, 2), lax.rem(r, 2)
    plane_peer = [lax.rem(j + d, J) for d in range(J)]
    in_plane = [{"fsdp": y * J + plane_peer[d]} for d in range(J)]
    along_y = [{"fsdp": lax.rem(y + t, Y) * J + j} for t in range(Y)]
    along_z = [{"rep": lax.rem(zh + q, Z) * 2 + core} for q in range(Z)]
    sibling = {"rep": zh * 2 + 1 - core}

    def remote(src, dst, send, recv, device):
        return pltpu.make_async_remote_copy(
            src_ref=src, dst_ref=dst, send_sem=send, recv_sem=recv, device_id=device, device_id_type=MESH
        )

    def rows(start, size):
        return pl.ds(pl.multiple_of(start, size), size)

    barrier = pltpu.get_barrier_semaphore()
    for device in in_plane[1:] + along_y[1:] + along_z[1:] + [sibling]:
        pl.semaphore_signal(barrier, inc=1, device_id=device, device_id_type=MESH)

    own_cots = pltpu.make_async_copy(cots, c_buf.at[rows(j * B, B)], cots_own)
    own_cots.start()

    def acts_block(k, target):
        return acts.at[:, rows((lax.rem(y + OFFSETS[k], Y) * J + target) * B, B)]

    own_acts = [
        pltpu.make_async_copy(acts_block(k, j), a_buf.at[rows(j * B, B), pl.ds(k * B, B)], acts_own.at[k])
        for k in range(Y)
    ]
    for copy in own_acts:
        copy.start()
    loads = [
        pltpu.make_async_copy(ref, state.at[i], state_sem.at[i])
        for i, ref in enumerate((inner, first, second, anchor, momentum))
    ]
    for load in loads:
        load.start()
    pl.semaphore_wait(barrier, J - 1 + Y - 1 + Z - 1 + 1)

    for d in range(1, J):
        remote(cots, c_buf.at[rows(j * B, B)], cots_s, cots_r, in_plane[d]).start()
    for k in range(Y):
        for d in range(1, J):
            remote(
                acts_block(k, plane_peer[d]), a_buf.at[rows(j * B, B), pl.ds(k * B, B)],
                acts_s.at[k], acts_r.at[k], in_plane[d],
            ).start()

    others = pl.ds(0, (J - 1) * B)
    all_cots = remote(c_buf.at[others], c_buf.at[others], cots_s, cots_r, in_plane[1])

    def acts_arrivals(k):
        block = a_buf.at[others, pl.ds(k * B, B)]
        return remote(block, block, acts_s.at[k], acts_r.at[k], in_plane[1])

    own_cots.wait()
    all_cots.wait_recv()

    def partial_gradient(k):
        own_acts[k].wait()
        acts_arrivals(k).wait_recv()
        return lax.dot_general(
            a_buf[:, pl.ds(k * B, B)], c_buf[...], (((0,), (0,)), ((), ())), preferred_element_type=F32
        )

    chain_cols = [pl.ds(s * (C // CHAIN), C // CHAIN) for s in range(CHAIN)]

    def chain(send_buf, recv_buf, send_sem, recv_sem, device):
        return [
            [
                remote(send_buf.at[i, :, cols], recv_buf.at[i, :, cols], send_sem.at[i, s], recv_sem.at[i, s], device)
                for s, cols in enumerate(chain_cols)
            ]
            for i in range(4)
        ]

    ups = chain(go_up, from_down, up_s, up_r, along_y[1])
    downs = chain(go_down, from_up, down_s, down_r, along_y[Y - 1])
    ups_first, downs_first = range(CHAIN // 2), range(CHAIN // 2, CHAIN)

    def add_and_send(i, part, copies, first_slices, send_buf, recv_buf):
        for s in range(CHAIN) if i else first_slices:
            cols = chain_cols[s]
            piece = part[:, s * (C // CHAIN) : (s + 1) * (C // CHAIN)]
            if i > 1 or i == 1 and s in first_slices:
                copies[i - 1][s].wait_recv()
                piece = piece + recv_buf[i - 1, :, cols].astype(F32)
            send_buf[i, :, cols] = piece.astype(BF16)
            copies[i][s].start()

    part = partial_gradient(SLOT[4])
    add_and_send(0, part, ups, ups_first, go_up, from_down)
    add_and_send(0, part, downs, downs_first, go_down, from_up)
    for i in range(1, 4):
        add_and_send(i, partial_gradient(SLOT[4 - i]), ups, ups_first, go_up, from_down)
        add_and_send(i, partial_gradient(SLOT[4 + i]), downs, downs_first, go_down, from_up)
    drift_buf[...] = partial_gradient(OWN)
    for load in loads:
        load.wait()

    H = B // 2
    W = C // SLICES
    slices = [pl.ds(s * W, W) for s in range(SLICES)]

    def inner_step(s):
        cols = slices[s]
        if s * CHAIN % SLICES == 0:
            ups[3][s * CHAIN // SLICES].wait_recv()
            downs[3][s * CHAIN // SLICES].wait_recv()
        gradient = drift_buf[:, cols] + from_down[3, :, cols].astype(F32) + from_up[3, :, cols].astype(F32)
        first_next = decay_first * state[1, :, cols] + (1.0 - decay_first) * gradient
        first_buf[:, cols] = first_next
        second_next = decay_second * state[2, :, cols] + (1.0 - decay_second) * gradient * gradient
        stepped = state[0, :, cols] - inner_rate * first_next / (jnp.sqrt(second_next) + epsilon)
        drift_buf[:, cols] = state[3, :, cols] - stepped
        pairs[s].start()

    pairs = [
        remote(drift_buf.at[rows((1 - core) * H, H), cols], drift_pair.at[:, cols], pair_s.at[s], pair_r.at[s], sibling)
        for s, cols in enumerate(slices)
    ]

    def z_copies(s):
        here = z_buf.at[zh, :, slices[s]]
        return [remote(here, here, z_s.at[s, q], z_r.at[s, q], along_z[q]) for q in range(1, Z)]

    zs = [z_copies(s) for s in range(SLICES)]

    def sum_cores(s):
        cols = slices[s]
        pairs[s].wait_recv()
        z_buf[zh, :, cols] = drift_buf[rows(core * H, H), cols] + drift_pair[:, cols]
        for copy in zs[s]:
            copy.start()

    def w_half(s, t, side):
        return w_buf.at[rows(SLOT[(Y - t) % Y] * B + side * H, H), slices[s]]

    near_first = (4, 3, 5, 2, 6, 1, 7)
    wys = [
        {t: remote(w_half(s, 0, core), w_half(s, t, core), wy_s.at[s, t], wy_r.at[s, t], along_y[t]) for t in near_first}
        for s in range(SLICES)
    ]
    forwards = [
        [remote(w_half(s, t, core), w_half(s, t, core), wc_s.at[s, t], wc_r.at[s, t], sibling) for t in range(Y)]
        for s in range(SLICES)
    ]

    def outer_step(s):
        cols = slices[s]
        for q in range(1, Z):
            there = z_buf.at[lax.rem(zh + Z - q, Z), :, cols]
            remote(there, there, z_s.at[s, q], z_r.at[s, q], along_z[q]).wait_recv()
        total = z_buf[0, :, cols] + z_buf[1, :, cols] + z_buf[2, :, cols] + z_buf[3, :, cols]
        average = total / (2 * Z)
        mine = rows(core * H, H)
        velocity = outer_decay * state[4, mine, cols] + average
        weights = state[3, mine, cols] - outer_rate * (average + outer_decay * velocity)
        w_buf[rows(OWN * B + core * H, H), cols] = weights.astype(BF16)
        for t in near_first:
            wys[s][t].start()
        forwards[s][0].start()

    def to_sibling(s):
        for t in reversed(near_first):
            wys[s][t].wait_recv()
            forwards[s][t].start()

    def values_of(s, d):
        return jnp.dot(a_buf[rows(plane_peer[d] * B, B), :], w_buf[:, slices[s]], preferred_element_type=F32)

    vs = [
        [remote(v_send.at[s, d], v_recv.at[s, d], v_s.at[s, d], v_r.at[s, d], in_plane[d]) for d in range(1, J)]
        for s in range(SLICES)
    ]

    def send_values(s):
        for t in range(Y):
            there = w_half(s, t, 1 - core)
            remote(there, there, wc_s.at[s, t], wc_r.at[s, t], sibling).wait_recv()
        for d in range(1, J):
            v_send[s, d] = values_of(s, d).astype(BF16)
            vs[s][d - 1].start()

    stores = [
        pltpu.make_async_copy(v_out.at[:, cols], values_out.at[:, cols], values_sem.at[s]) for s, cols in enumerate(slices)
    ]

    def sum_values(s):
        total = values_of(s, 0)
        for d in range(1, J):
            vs[s][d - 1].wait_recv()
            total = total + v_recv[s, d].astype(F32)
        v_out[:, slices[s]] = total.astype(BF16)
        stores[s].start()

    for s in range(SLICES):
        inner_step(s)
        if s:
            sum_cores(s - 1)
    sum_cores(SLICES - 1)
    store_first = pltpu.make_async_copy(first_buf, first_out, first_sem)
    store_first.start()
    for s in range(SLICES):
        outer_step(s)
    for s in range(SLICES):
        to_sibling(s)
        send_values(s)
    for s in range(SLICES):
        sum_values(s)

    all_cots.wait_send()
    for k in range(Y):
        acts_arrivals(k).wait_send()
    for copies, first_slices in ((ups, ups_first), (downs, downs_first)):
        for i in range(4):
            for s in range(CHAIN) if i else first_slices:
                copies[i][s].wait_send()
    for s in range(SLICES):
        for copy in [pairs[s]] + zs[s] + list(wys[s].values()) + forwards[s] + vs[s]:
            copy.wait_send()
    store_first.wait()
    for store in stores:
        store.wait()


def on_device(acts, value_cots, inner_weights, first_moment, second_moment, anchor, outer_momentum):
    dma = pltpu.SemaphoreType.DMA
    vmem = pltpu.VMEM
    first_next, values = pl.pallas_call(
        step_kernel,
        name="diloco_step",
        out_shape=(jax.ShapeDtypeStruct((B, C), F32), jax.ShapeDtypeStruct((B, C), BF16)),
        in_specs=[pl.BlockSpec(memory_space=pl.ANY)] * 7,
        out_specs=(pl.BlockSpec(memory_space=pl.ANY), pl.BlockSpec(memory_space=pl.ANY)),
        scratch_shapes=[
            vmem((J * B, Y * B), BF16),
            vmem((J * B, C), BF16),
            vmem((5, B, C), F32),
            vmem((B, C), F32),
            vmem((4, B, C), BF16),
            vmem((4, B, C), BF16),
            vmem((4, B, C), BF16),
            vmem((4, B, C), BF16),
            vmem((B, C), F32),
            vmem((B // 2, C), F32),
            vmem((Z, B // 2, C), F32),
            vmem((Y * B, C), BF16),
            vmem((SLICES, J, B, C // SLICES), BF16),
            vmem((SLICES, J, B, C // SLICES), BF16),
            vmem((B, C), BF16),
            dma((5,)),
            dma(()), dma(()), dma(()),
            dma((Y,)), dma((Y,)), dma((Y,)),
            dma((4, CHAIN)), dma((4, CHAIN)), dma((4, CHAIN)), dma((4, CHAIN)),
            dma((SLICES,)), dma((SLICES,)),
            dma((SLICES, Z)), dma((SLICES, Z)),
            dma((SLICES, Y)), dma((SLICES, Y)),
            dma((SLICES, Y)), dma((SLICES, Y)),
            dma((SLICES, J)), dma((SLICES, J)),
            dma(()), dma((SLICES,)),
        ],
        compiler_params=pltpu.CompilerParams(
            collective_id=0, has_side_effects=True, vmem_limit_bytes=62 * 1024 * 1024
        ),
    )(acts[0], value_cots[0], inner_weights[0], first_moment[0], second_moment[0], anchor, outer_momentum)
    return first_next[None], values[None]


def solution(mesh):
    placed = (
        P("rep", "fsdp", None),
        P("rep", "fsdp", None),
        P("rep", "fsdp", None),
        P("rep", "fsdp", None),
        P("rep", "fsdp", None),
        P("fsdp", None),
        P("fsdp", None),
    )
    return jax.shard_map(
        on_device,
        mesh=mesh,
        in_specs=placed,
        out_specs=(P("rep", "fsdp", None), P("rep", "fsdp", None)),
        check_vma=False,
    )
```

```python
import jax
import jax.numpy as jnp
from jax import lax
from jax.experimental import pallas as pl
from jax.experimental.pallas import tpu as pltpu
from jax.sharding import PartitionSpec as P

decay_first = 0.9
decay_second = 0.95
inner_rate = 0.006
epsilon = 1e-08
outer_rate = 0.7
outer_decay = 0.9

MESH = pl.DeviceIdType.MESH
F32 = jnp.float32
BF16 = jnp.bfloat16

Y = 8
J = 8
Z = 4
B = 128
C = 512
OFFSETS = (4, 3, 5, 2, 6, 1, 7, 0)
SLOT = {off: k for k, off in enumerate(OFFSETS)}
OWN = SLOT[0]
EARLY = 1
CHAIN = 2
SLICES = 4


def step_kernel(
    acts, cots, inner, first, second, anchor, momentum, first_out, values_out,
    a_buf, c_buf, state, first_buf, go_up, go_down, from_down, from_up,
    drift_buf, drift_pair, z_buf, w_buf, v_send, v_recv, v_out,
    state_sem, cots_own, cots_s, cots_r, acts_own, acts_s, acts_r, up_s, up_r, down_s, down_r,
    pair_s, pair_r, z_s, z_r, wy_s, wy_r, wc_s, wc_r, v_s, v_r, first_sem, values_sem,
):
    f = lax.axis_index("fsdp")
    r = lax.axis_index("rep")
    y, j = lax.div(f, J), lax.rem(f, J)
    zh, core = lax.div(r, 2), lax.rem(r, 2)
    plane_peer = [lax.rem(j + d, J) for d in range(J)]
    in_plane = [{"fsdp": y * J + plane_peer[d]} for d in range(J)]
    along_y = [{"fsdp": lax.rem(y + t, Y) * J + j} for t in range(Y)]
    along_z = [{"rep": lax.rem(zh + q, Z) * 2 + core} for q in range(Z)]
    sibling = {"rep": zh * 2 + 1 - core}

    def remote(src, dst, send, recv, device):
        return pltpu.make_async_remote_copy(
            src_ref=src, dst_ref=dst, send_sem=send, recv_sem=recv, device_id=device, device_id_type=MESH
        )

    def rows(start, size):
        return pl.ds(pl.multiple_of(start, size), size)

    barrier = pltpu.get_barrier_semaphore()
    for device in in_plane[1:] + along_y[1:] + along_z[1:] + [sibling]:
        pl.semaphore_signal(barrier, inc=1, device_id=device, device_id_type=MESH)

    own_cots = pltpu.make_async_copy(cots, c_buf.at[rows(j * B, B)], cots_own)
    own_cots.start()

    def acts_block(k, target):
        return acts.at[:, rows((lax.rem(y + OFFSETS[k], Y) * J + target) * B, B)]

    own_acts = [
        pltpu.make_async_copy(acts_block(k, j), a_buf.at[rows(j * B, B), pl.ds(k * B, B)], acts_own.at[k])
        for k in range(Y)
    ]
    for copy in own_acts:
        copy.start()
    loads = [
        pltpu.make_async_copy(ref, state.at[i], state_sem.at[i])
        for i, ref in enumerate((inner, first, second, anchor, momentum))
    ]
    for load in loads:
        load.start()
    pl.semaphore_wait(barrier, J - 1 + Y - 1 + Z - 1 + 1)

    def send_acts(k):
        for d in range(1, J):
            remote(
                acts_block(k, plane_peer[d]), a_buf.at[rows(j * B, B), pl.ds(k * B, B)],
                acts_s.at[k], acts_r.at[k], in_plane[d],
            ).start()

    half = C // 2
    z_piece = j + 1 - 2 * lax.rem(j, 2)
    z_partner = {"fsdp": y * J + z_piece}
    along_x = (2, 4, 6)

    def cots_piece(owner, cols):
        return c_buf.at[rows(owner * B, B), cols]

    every, low_cols, high_cols = pl.ds(0, C), pl.ds(0, half), pl.ds(half, half)
    own_piece = cots_piece(j, every)
    remote(cots, own_piece, cots_s.at[0], cots_r.at[0], z_partner).start()
    for d in along_x:
        remote(cots, own_piece, cots_s.at[1], cots_r.at[1], in_plane[d]).start()
    for k in range(EARLY):
        send_acts(k)
    three = pl.ds(0, len(along_x) * B)
    cots_groups = [
        remote(c_buf.at[r, c], c_buf.at[r, c], cots_s.at[i], cots_r.at[i], z_partner)
        for i, (r, c) in enumerate(
            ((pl.ds(0, B), every), (three, every), (three, low_cols), (three, high_cols))
        )
    ]
    cots_groups[0].wait_recv()
    for d in along_x:
        piece = cots_piece(z_piece, high_cols)
        remote(piece, piece, cots_s.at[3], cots_r.at[3], in_plane[d]).start()
    cots_groups[1].wait_recv()
    for d in along_x:
        piece = cots_piece(plane_peer[d], low_cols)
        remote(piece, piece, cots_s.at[2], cots_r.at[2], z_partner).start()
    for k in range(EARLY, Y):
        send_acts(k)

    others = pl.ds(0, (J - 1) * B)

    def acts_arrivals(k):
        block = a_buf.at[others, pl.ds(k * B, B)]
        return remote(block, block, acts_s.at[k], acts_r.at[k], in_plane[1])

    own_cots.wait()
    cots_groups[2].wait_recv()
    cots_groups[3].wait_recv()

    def partial_gradient(k):
        own_acts[k].wait()
        acts_arrivals(k).wait_recv()
        return lax.dot_general(
            a_buf[:, pl.ds(k * B, B)], c_buf[...], (((0,), (0,)), ((), ())), preferred_element_type=F32
        )

    chain_cols = [pl.ds(s * (C // CHAIN), C // CHAIN) for s in range(CHAIN)]

    def chain(send_buf, recv_buf, send_sem, recv_sem, device):
        return [
            [
                remote(send_buf.at[i, :, cols], recv_buf.at[i, :, cols], send_sem.at[i, s], recv_sem.at[i, s], device)
                for s, cols in enumerate(chain_cols)
            ]
            for i in range(4)
        ]

    ups = chain(go_up, from_down, up_s, up_r, along_y[1])
    downs = chain(go_down, from_up, down_s, down_r, along_y[Y - 1])
    ups_first, downs_first = range(CHAIN // 2), range(CHAIN // 2, CHAIN)

    def add_and_send(i, part, copies, first_slices, send_buf, recv_buf):
        for s in range(CHAIN) if i else first_slices:
            cols = chain_cols[s]
            piece = part[:, s * (C // CHAIN) : (s + 1) * (C // CHAIN)]
            if i > 1 or i == 1 and s in first_slices:
                copies[i - 1][s].wait_recv()
                piece = piece + recv_buf[i - 1, :, cols].astype(F32)
            send_buf[i, :, cols] = piece.astype(BF16)
            copies[i][s].start()

    part = partial_gradient(SLOT[4])
    add_and_send(0, part, ups, ups_first, go_up, from_down)
    add_and_send(0, part, downs, downs_first, go_down, from_up)
    for i in range(1, 4):
        add_and_send(i, partial_gradient(SLOT[4 - i]), ups, ups_first, go_up, from_down)
        add_and_send(i, partial_gradient(SLOT[4 + i]), downs, downs_first, go_down, from_up)
    drift_buf[...] = partial_gradient(OWN)
    for load in loads:
        load.wait()

    H = B // 2
    W = C // SLICES
    slices = [pl.ds(s * W, W) for s in range(SLICES)]

    def inner_step(s):
        cols = slices[s]
        if s * CHAIN % SLICES == 0:
            ups[3][s * CHAIN // SLICES].wait_recv()
            downs[3][s * CHAIN // SLICES].wait_recv()
        gradient = drift_buf[:, cols] + from_down[3, :, cols].astype(F32) + from_up[3, :, cols].astype(F32)
        first_next = decay_first * state[1, :, cols] + (1.0 - decay_first) * gradient
        first_buf[:, cols] = first_next
        second_next = decay_second * state[2, :, cols] + (1.0 - decay_second) * gradient * gradient
        stepped = state[0, :, cols] - inner_rate * first_next / (jnp.sqrt(second_next) + epsilon)
        drift_buf[:, cols] = state[3, :, cols] - stepped
        pairs[s].start()

    pairs = [
        remote(drift_buf.at[rows((1 - core) * H, H), cols], drift_pair.at[:, cols], pair_s.at[s], pair_r.at[s], sibling)
        for s, cols in enumerate(slices)
    ]

    def z_copies(s):
        here = z_buf.at[zh, :, slices[s]]
        return [remote(here, here, z_s.at[s, q], z_r.at[s, q], along_z[q]) for q in range(1, Z)]

    zs = [z_copies(s) for s in range(SLICES)]

    def sum_cores(s):
        cols = slices[s]
        pairs[s].wait_recv()
        z_buf[zh, :, cols] = (drift_buf[rows(core * H, H), cols] + drift_pair[:, cols]).astype(BF16)
        for copy in zs[s]:
            copy.start()

    def w_half(s, t, side):
        return w_buf.at[rows(SLOT[(Y - t) % Y] * B + side * H, H), slices[s]]

    near_first = (4, 3, 5, 2, 6, 1, 7)
    wys = [
        {t: remote(w_half(s, 0, core), w_half(s, t, core), wy_s.at[s, t], wy_r.at[s, t], along_y[t]) for t in near_first}
        for s in range(SLICES)
    ]
    forwards = [
        [remote(w_half(s, t, core), w_half(s, t, core), wc_s.at[s, t], wc_r.at[s, t], sibling) for t in range(Y)]
        for s in range(SLICES)
    ]

    def outer_step(s):
        cols = slices[s]
        for q in range(1, Z):
            there = z_buf.at[lax.rem(zh + Z - q, Z), :, cols]
            remote(there, there, z_s.at[s, q], z_r.at[s, q], along_z[q]).wait_recv()
        sums = [z_buf[q, :, cols].astype(F32) for q in range(Z)]
        total = sums[0] + sums[1] + sums[2] + sums[3]
        average = total / (2 * Z)
        mine = rows(core * H, H)
        velocity = outer_decay * state[4, mine, cols] + average
        weights = state[3, mine, cols] - outer_rate * (average + outer_decay * velocity)
        w_buf[rows(OWN * B + core * H, H), cols] = weights.astype(BF16)
        for t in near_first:
            wys[s][t].start()
        forwards[s][0].start()

    def to_sibling(s):
        for t in reversed(near_first):
            wys[s][t].wait_recv()
            forwards[s][t].start()

    def values_of(s, d):
        return jnp.dot(a_buf[rows(plane_peer[d] * B, B), :], w_buf[:, slices[s]], preferred_element_type=F32)

    vs = [
        [remote(v_send.at[s, d], v_recv.at[s, d], v_s.at[s, d], v_r.at[s, d], in_plane[d]) for d in range(1, J)]
        for s in range(SLICES)
    ]

    def send_values(s):
        for t in range(Y):
            there = w_half(s, t, 1 - core)
            remote(there, there, wc_s.at[s, t], wc_r.at[s, t], sibling).wait_recv()
        for d in range(1, J):
            v_send[s, d] = values_of(s, d).astype(BF16)
            vs[s][d - 1].start()

    stores = [
        pltpu.make_async_copy(v_out.at[:, cols], values_out.at[:, cols], values_sem.at[s]) for s, cols in enumerate(slices)
    ]

    def sum_values(s):
        total = values_of(s, 0)
        for d in range(1, J):
            vs[s][d - 1].wait_recv()
            total = total + v_recv[s, d].astype(F32)
        v_out[:, slices[s]] = total.astype(BF16)
        stores[s].start()

    for s in range(SLICES):
        inner_step(s)
        if s:
            sum_cores(s - 1)
    sum_cores(SLICES - 1)
    store_first = pltpu.make_async_copy(first_buf, first_out, first_sem)
    store_first.start()
    for s in range(SLICES):
        outer_step(s)
    for s in range(SLICES):
        to_sibling(s)
        send_values(s)
    for s in range(SLICES):
        sum_values(s)

    for copies in cots_groups:
        copies.wait_send()
    for k in range(Y):
        acts_arrivals(k).wait_send()
    for copies, first_slices in ((ups, ups_first), (downs, downs_first)):
        for i in range(4):
            for s in range(CHAIN) if i else first_slices:
                copies[i][s].wait_send()
    for s in range(SLICES):
        for copy in [pairs[s]] + zs[s] + list(wys[s].values()) + forwards[s] + vs[s]:
            copy.wait_send()
    store_first.wait()
    for store in stores:
        store.wait()


def on_device(acts, value_cots, inner_weights, first_moment, second_moment, anchor, outer_momentum):
    dma = pltpu.SemaphoreType.DMA
    vmem = pltpu.VMEM
    first_next, values = pl.pallas_call(
        step_kernel,
        name="diloco_step",
        out_shape=(jax.ShapeDtypeStruct((B, C), F32), jax.ShapeDtypeStruct((B, C), BF16)),
        in_specs=[pl.BlockSpec(memory_space=pl.ANY)] * 7,
        out_specs=(pl.BlockSpec(memory_space=pl.ANY), pl.BlockSpec(memory_space=pl.ANY)),
        scratch_shapes=[
            vmem((J * B, Y * B), BF16),
            vmem((J * B, C), BF16),
            vmem((5, B, C), F32),
            vmem((B, C), F32),
            vmem((4, B, C), BF16),
            vmem((4, B, C), BF16),
            vmem((4, B, C), BF16),
            vmem((4, B, C), BF16),
            vmem((B, C), F32),
            vmem((B // 2, C), F32),
            vmem((Z, B // 2, C), BF16),
            vmem((Y * B, C), BF16),
            vmem((SLICES, J, B, C // SLICES), BF16),
            vmem((SLICES, J, B, C // SLICES), BF16),
            vmem((B, C), BF16),
            dma((5,)),
            dma(()), dma((4,)), dma((4,)),
            dma((Y,)), dma((Y,)), dma((Y,)),
            dma((4, CHAIN)), dma((4, CHAIN)), dma((4, CHAIN)), dma((4, CHAIN)),
            dma((SLICES,)), dma((SLICES,)),
            dma((SLICES, Z)), dma((SLICES, Z)),
            dma((SLICES, Y)), dma((SLICES, Y)),
            dma((SLICES, Y)), dma((SLICES, Y)),
            dma((SLICES, J)), dma((SLICES, J)),
            dma(()), dma((SLICES,)),
        ],
        compiler_params=pltpu.CompilerParams(
            collective_id=0, has_side_effects=True, vmem_limit_bytes=62 * 1024 * 1024
        ),
    )(acts[0], value_cots[0], inner_weights[0], first_moment[0], second_moment[0], anchor, outer_momentum)
    return first_next[None], values[None]


def solution(mesh):
    placed = (
        P("rep", "fsdp", None),
        P("rep", "fsdp", None),
        P("rep", "fsdp", None),
        P("rep", "fsdp", None),
        P("rep", "fsdp", None),
        P("fsdp", None),
        P("fsdp", None),
    )
    return jax.shard_map(
        on_device,
        mesh=mesh,
        in_specs=placed,
        out_specs=(P("rep", "fsdp", None), P("rep", "fsdp", None)),
        check_vma=False,
    )
```

```python
import jax
import jax.numpy as jnp
from jax import lax
from jax.experimental import pallas as pl
from jax.experimental.pallas import tpu as pltpu
from jax.sharding import PartitionSpec as P

decay_first = 0.9
decay_second = 0.95
inner_rate = 0.006
epsilon = 1e-08
outer_rate = 0.7
outer_decay = 0.9

MESH = pl.DeviceIdType.MESH
F32 = jnp.float32
BF16 = jnp.bfloat16

Y = 8
J = 8
Z = 4
B = 128
C = 512
OFFSETS = (4, 3, 5, 2, 6, 1, 7, 0)
SLOT = {off: k for k, off in enumerate(OFFSETS)}
OWN = SLOT[0]
EARLY = 1
CHAIN = 2
SLICES = 4


def step_kernel(
    acts, cots, inner, first, second, anchor, momentum, first_out, values_out,
    a_buf, c_buf, state, first_buf, go_up, go_down, from_down, from_up,
    stepped_buf, stepped_pair, z_buf, w_buf, v_send, v_recv, v_out,
    state_sem, cots_own, cots_s, cots_r, acts_own, acts_s, acts_r, up_s, up_r, down_s, down_r,
    pair_s, pair_r, z_s, z_r, wy_s, wy_r, wc_s, wc_r, v_s, v_r, first_sem, values_sem,
):
    f = lax.axis_index("fsdp")
    r = lax.axis_index("rep")
    y, j = lax.div(f, J), lax.rem(f, J)
    zh, core = lax.div(r, 2), lax.rem(r, 2)
    plane_peer = [lax.rem(j + d, J) for d in range(J)]
    in_plane = [{"fsdp": y * J + plane_peer[d]} for d in range(J)]
    along_y = [{"fsdp": lax.rem(y + t, Y) * J + j} for t in range(Y)]
    along_z = [{"rep": lax.rem(zh + q, Z) * 2 + core} for q in range(Z)]
    sibling = {"rep": zh * 2 + 1 - core}

    def remote(src, dst, send, recv, device):
        return pltpu.make_async_remote_copy(
            src_ref=src, dst_ref=dst, send_sem=send, recv_sem=recv, device_id=device, device_id_type=MESH
        )

    def rows(start, size):
        return pl.ds(pl.multiple_of(start, size), size)

    barrier = pltpu.get_barrier_semaphore()
    for device in in_plane[1:] + along_y[1:] + along_z[1:] + [sibling]:
        pl.semaphore_signal(barrier, inc=1, device_id=device, device_id_type=MESH)

    own_cots = pltpu.make_async_copy(cots, c_buf.at[rows(j * B, B)], cots_own)
    own_cots.start()

    def acts_block(k, target):
        return acts.at[:, rows((lax.rem(y + OFFSETS[k], Y) * J + target) * B, B)]

    own_acts = [
        pltpu.make_async_copy(acts_block(k, j), a_buf.at[rows(j * B, B), pl.ds(k * B, B)], acts_own.at[k])
        for k in range(Y)
    ]
    for copy in own_acts:
        copy.start()
    loads = [
        pltpu.make_async_copy(ref, state.at[i], state_sem.at[i])
        for i, ref in enumerate((inner, first, second, anchor, momentum))
    ]
    for load in loads:
        load.start()
    pl.semaphore_wait(barrier, J - 1 + Y - 1 + Z - 1 + 1)

    def send_acts(k):
        for d in range(1, J):
            remote(
                acts_block(k, plane_peer[d]), a_buf.at[rows(j * B, B), pl.ds(k * B, B)],
                acts_s.at[k], acts_r.at[k], in_plane[d],
            ).start()

    half = C // 2
    z_piece = j + 1 - 2 * lax.rem(j, 2)
    z_partner = {"fsdp": y * J + z_piece}
    along_x = (2, 4, 6)

    def cots_piece(owner, cols):
        return c_buf.at[rows(owner * B, B), cols]

    every, low_cols, high_cols = pl.ds(0, C), pl.ds(0, half), pl.ds(half, half)
    own_piece = cots_piece(j, every)
    remote(cots, own_piece, cots_s.at[0], cots_r.at[0], z_partner).start()
    for d in along_x:
        remote(cots, own_piece, cots_s.at[1], cots_r.at[1], in_plane[d]).start()
    for k in range(EARLY):
        send_acts(k)
    three = pl.ds(0, len(along_x) * B)
    cots_groups = [
        remote(c_buf.at[r, c], c_buf.at[r, c], cots_s.at[i], cots_r.at[i], z_partner)
        for i, (r, c) in enumerate(
            ((pl.ds(0, B), every), (three, every), (three, low_cols), (three, high_cols))
        )
    ]
    cots_groups[0].wait_recv()
    for d in along_x:
        piece = cots_piece(z_piece, high_cols)
        remote(piece, piece, cots_s.at[3], cots_r.at[3], in_plane[d]).start()
    cots_groups[1].wait_recv()
    for d in along_x:
        piece = cots_piece(plane_peer[d], low_cols)
        remote(piece, piece, cots_s.at[2], cots_r.at[2], z_partner).start()
    for k in range(EARLY, Y):
        send_acts(k)

    others = pl.ds(0, (J - 1) * B)

    def acts_arrivals(k):
        block = a_buf.at[others, pl.ds(k * B, B)]
        return remote(block, block, acts_s.at[k], acts_r.at[k], in_plane[1])

    own_cots.wait()
    cots_groups[2].wait_recv()
    cots_groups[3].wait_recv()

    def partial_gradient(k):
        own_acts[k].wait()
        acts_arrivals(k).wait_recv()
        return lax.dot_general(
            a_buf[:, pl.ds(k * B, B)], c_buf[...], (((0,), (0,)), ((), ())), preferred_element_type=F32
        )

    chain_cols = [pl.ds(s * (C // CHAIN), C // CHAIN) for s in range(CHAIN)]

    def chain(send_buf, recv_buf, send_sem, recv_sem, device):
        return [
            [
                remote(send_buf.at[i, :, cols], recv_buf.at[i, :, cols], send_sem.at[i, s], recv_sem.at[i, s], device)
                for s, cols in enumerate(chain_cols)
            ]
            for i in range(4)
        ]

    ups = chain(go_up, from_down, up_s, up_r, along_y[1])
    downs = chain(go_down, from_up, down_s, down_r, along_y[Y - 1])
    ups_first, downs_first = range(CHAIN // 2), range(CHAIN // 2, CHAIN)

    def add_and_send(i, part, copies, first_slices, send_buf, recv_buf):
        for s in range(CHAIN) if i else first_slices:
            cols = chain_cols[s]
            piece = part[:, s * (C // CHAIN) : (s + 1) * (C // CHAIN)]
            if i > 1 or i == 1 and s in first_slices:
                copies[i - 1][s].wait_recv()
                piece = piece + recv_buf[i - 1, :, cols].astype(F32)
            send_buf[i, :, cols] = piece.astype(BF16)
            copies[i][s].start()

    part = partial_gradient(SLOT[4])
    add_and_send(0, part, ups, ups_first, go_up, from_down)
    add_and_send(0, part, downs, downs_first, go_down, from_up)
    for i in range(1, 4):
        add_and_send(i, partial_gradient(SLOT[4 - i]), ups, ups_first, go_up, from_down)
        add_and_send(i, partial_gradient(SLOT[4 + i]), downs, downs_first, go_down, from_up)
    own_acts[OWN].wait()
    acts_arrivals(OWN).wait_recv()
    own_block = a_buf[:, pl.ds(OWN * B, B)].T
    for load in loads:
        load.wait()

    H = B // 2
    W = C // SLICES
    slices = [pl.ds(s * W, W) for s in range(SLICES)]

    def inner_step(s):
        cols = slices[s]
        if s * CHAIN % SLICES == 0:
            ups[3][s * CHAIN // SLICES].wait_recv()
            downs[3][s * CHAIN // SLICES].wait_recv()
        part = jnp.dot(own_block, c_buf[:, cols], preferred_element_type=F32)
        gradient = part + from_down[3, :, cols].astype(F32) + from_up[3, :, cols].astype(F32)
        first_next = decay_first * state[1, :, cols] + (1.0 - decay_first) * gradient
        first_buf[:, cols] = first_next
        second_next = decay_second * state[2, :, cols] + (1.0 - decay_second) * gradient * gradient
        stepped = state[0, :, cols] - inner_rate * first_next / (jnp.sqrt(second_next) + epsilon)
        stepped_buf[:, cols] = stepped
        pairs[s].start()

    pairs = [
        remote(stepped_buf.at[rows((1 - core) * H, H), cols], stepped_pair.at[:, cols], pair_s.at[s], pair_r.at[s], sibling)
        for s, cols in enumerate(slices)
    ]

    def z_copies(s):
        here = z_buf.at[zh, :, slices[s]]
        return [remote(here, here, z_s.at[s, q], z_r.at[s, q], along_z[q]) for q in range(1, Z)]

    zs = [z_copies(s) for s in range(SLICES)]

    def sum_cores(s):
        cols = slices[s]
        pairs[s].wait_recv()
        z_buf[zh, :, cols] = (stepped_buf[rows(core * H, H), cols] + stepped_pair[:, cols]).astype(BF16)
        for copy in zs[s]:
            copy.start()

    def w_half(s, t, side):
        return w_buf.at[rows(SLOT[(Y - t) % Y] * B + side * H, H), slices[s]]

    near_first = (4, 3, 5, 2, 6, 1, 7)
    wys = [
        {t: remote(w_half(s, 0, core), w_half(s, t, core), wy_s.at[s, t], wy_r.at[s, t], along_y[t]) for t in near_first}
        for s in range(SLICES)
    ]
    forwards = [
        [remote(w_half(s, t, core), w_half(s, t, core), wc_s.at[s, t], wc_r.at[s, t], sibling) for t in range(Y)]
        for s in range(SLICES)
    ]

    def outer_step(s):
        cols = slices[s]
        for q in range(1, Z):
            there = z_buf.at[lax.rem(zh + Z - q, Z), :, cols]
            remote(there, there, z_s.at[s, q], z_r.at[s, q], along_z[q]).wait_recv()
        sums = [z_buf[q, :, cols].astype(F32) for q in range(Z)]
        total = sums[0] + sums[1] + sums[2] + sums[3]
        mine = rows(core * H, H)
        average = state[3, mine, cols] - total / (2 * Z)
        velocity = outer_decay * state[4, mine, cols] + average
        weights = state[3, mine, cols] - outer_rate * (average + outer_decay * velocity)
        w_buf[rows(OWN * B + core * H, H), cols] = weights.astype(BF16)
        for t in near_first:
            wys[s][t].start()
        forwards[s][0].start()

    def to_sibling(s):
        for t in reversed(near_first):
            wys[s][t].wait_recv()
            forwards[s][t].start()

    def values_of(s, d):
        return jnp.dot(a_buf[rows(plane_peer[d] * B, B), :], w_buf[:, slices[s]], preferred_element_type=F32)

    vs = [
        [remote(v_send.at[s, d], v_recv.at[s, d], v_s.at[s, d], v_r.at[s, d], in_plane[d]) for d in range(1, J)]
        for s in range(SLICES)
    ]

    def send_values(s):
        for t in range(Y):
            there = w_half(s, t, 1 - core)
            remote(there, there, wc_s.at[s, t], wc_r.at[s, t], sibling).wait_recv()
        for d in range(1, J):
            v_send[s, d] = values_of(s, d).astype(BF16)
            vs[s][d - 1].start()

    stores = [
        pltpu.make_async_copy(v_out.at[:, cols], values_out.at[:, cols], values_sem.at[s]) for s, cols in enumerate(slices)
    ]

    def sum_values(s):
        total = values_of(s, 0)
        for d in range(1, J):
            vs[s][d - 1].wait_recv()
            total = total + v_recv[s, d].astype(F32)
        v_out[:, slices[s]] = total.astype(BF16)
        stores[s].start()

    for s in range(SLICES):
        inner_step(s)
        sum_cores(s)
    store_first = pltpu.make_async_copy(first_buf, first_out, first_sem)
    store_first.start()
    for s in range(SLICES):
        outer_step(s)
    for s in range(SLICES):
        to_sibling(s)
        send_values(s)
    for s in range(SLICES):
        sum_values(s)

    for copies in cots_groups:
        copies.wait_send()
    for k in range(Y):
        acts_arrivals(k).wait_send()
    for copies, first_slices in ((ups, ups_first), (downs, downs_first)):
        for i in range(4):
            for s in range(CHAIN) if i else first_slices:
                copies[i][s].wait_send()
    for s in range(SLICES):
        for copy in [pairs[s]] + zs[s] + list(wys[s].values()) + forwards[s] + vs[s]:
            copy.wait_send()
    store_first.wait()
    for store in stores:
        store.wait()


def on_device(acts, value_cots, inner_weights, first_moment, second_moment, anchor, outer_momentum):
    dma = pltpu.SemaphoreType.DMA
    vmem = pltpu.VMEM
    first_next, values = pl.pallas_call(
        step_kernel,
        name="diloco_step",
        out_shape=(jax.ShapeDtypeStruct((B, C), F32), jax.ShapeDtypeStruct((B, C), BF16)),
        in_specs=[pl.BlockSpec(memory_space=pl.ANY)] * 7,
        out_specs=(pl.BlockSpec(memory_space=pl.ANY), pl.BlockSpec(memory_space=pl.ANY)),
        scratch_shapes=[
            vmem((J * B, Y * B), BF16),
            vmem((J * B, C), BF16),
            vmem((5, B, C), F32),
            vmem((B, C), F32),
            vmem((4, B, C), BF16),
            vmem((4, B, C), BF16),
            vmem((4, B, C), BF16),
            vmem((4, B, C), BF16),
            vmem((B, C), F32),
            vmem((B // 2, C), F32),
            vmem((Z, B // 2, C), BF16),
            vmem((Y * B, C), BF16),
            vmem((SLICES, J, B, C // SLICES), BF16),
            vmem((SLICES, J, B, C // SLICES), BF16),
            vmem((B, C), BF16),
            dma((5,)),
            dma(()), dma((4,)), dma((4,)),
            dma((Y,)), dma((Y,)), dma((Y,)),
            dma((4, CHAIN)), dma((4, CHAIN)), dma((4, CHAIN)), dma((4, CHAIN)),
            dma((SLICES,)), dma((SLICES,)),
            dma((SLICES, Z)), dma((SLICES, Z)),
            dma((SLICES, Y)), dma((SLICES, Y)),
            dma((SLICES, Y)), dma((SLICES, Y)),
            dma((SLICES, J)), dma((SLICES, J)),
            dma(()), dma((SLICES,)),
        ],
        compiler_params=pltpu.CompilerParams(
            collective_id=0, has_side_effects=True, vmem_limit_bytes=62 * 1024 * 1024
        ),
    )(acts[0], value_cots[0], inner_weights[0], first_moment[0], second_moment[0], anchor, outer_momentum)
    return first_next[None], values[None]


def solution(mesh):
    placed = (
        P("rep", "fsdp", None),
        P("rep", "fsdp", None),
        P("rep", "fsdp", None),
        P("rep", "fsdp", None),
        P("rep", "fsdp", None),
        P("fsdp", None),
        P("fsdp", None),
    )
    return jax.shard_map(
        on_device,
        mesh=mesh,
        in_specs=placed,
        out_specs=(P("rep", "fsdp", None), P("rep", "fsdp", None)),
        check_vma=False,
    )
```

```python
import jax
import jax.numpy as jnp
from jax import lax
from jax.experimental import pallas as pl
from jax.experimental.pallas import tpu as pltpu
from jax.sharding import PartitionSpec as P

decay_first = 0.9
decay_second = 0.95
inner_rate = 0.006
epsilon = 1e-08
outer_rate = 0.7
outer_decay = 0.9

MESH = pl.DeviceIdType.MESH
F32 = jnp.float32
BF16 = jnp.bfloat16

Y = 8
J = 8
Z = 4
B = 128
C = 512
OFFSETS = (4, 3, 5, 2, 6, 1, 7, 0)
SLOT = {off: k for k, off in enumerate(OFFSETS)}
OWN = SLOT[0]
EARLY = 1
CHAIN = 2
SLICES = 4


def step_kernel(
    acts, cots, inner, first, second, anchor, momentum, first_out, values_out,
    a_buf, c_buf, state, first_buf, go_up, go_down, from_down, from_up,
    stepped_buf, stepped_pair, z_buf, w_buf, v_send, v_recv, v_out,
    state_sem, cots_own, cots_s, cots_r, acts_own, acts_s, acts_r, up_s, up_r, down_s, down_r,
    pair_s, pair_r, z_s, z_r, wy_s, wy_r, wc_s, wc_r, v_s, v_r, first_sem, values_sem,
):
    f = lax.axis_index("fsdp")
    r = lax.axis_index("rep")
    y, j = lax.div(f, J), lax.rem(f, J)
    zh, core = lax.div(r, 2), lax.rem(r, 2)
    plane_peer = [lax.rem(j + d, J) for d in range(J)]
    in_plane = [{"fsdp": y * J + plane_peer[d]} for d in range(J)]
    along_y = [{"fsdp": lax.rem(y + t, Y) * J + j} for t in range(Y)]
    along_z = [{"rep": lax.rem(zh + q, Z) * 2 + core} for q in range(Z)]
    sibling = {"rep": zh * 2 + 1 - core}

    def remote(src, dst, send, recv, device):
        return pltpu.make_async_remote_copy(
            src_ref=src, dst_ref=dst, send_sem=send, recv_sem=recv, device_id=device, device_id_type=MESH
        )

    def rows(start, size):
        return pl.ds(pl.multiple_of(start, size), size)

    barrier = pltpu.get_barrier_semaphore()
    for device in in_plane[1:] + along_y[1:] + along_z[1:] + [sibling]:
        pl.semaphore_signal(barrier, inc=1, device_id=device, device_id_type=MESH)

    own_cots = pltpu.make_async_copy(cots, c_buf.at[rows(j * B, B)], cots_own)
    own_cots.start()

    def acts_block(k, target):
        return acts.at[:, rows((lax.rem(y + OFFSETS[k], Y) * J + target) * B, B)]

    own_acts = [
        pltpu.make_async_copy(acts_block(k, j), a_buf.at[rows(j * B, B), pl.ds(k * B, B)], acts_own.at[k])
        for k in range(Y)
    ]
    for copy in own_acts:
        copy.start()
    loads = [
        pltpu.make_async_copy(ref, state.at[i], state_sem.at[i])
        for i, ref in enumerate((inner, first, second, anchor, momentum))
    ]
    for load in loads:
        load.start()
    pl.semaphore_wait(barrier, J - 1 + Y - 1 + Z - 1 + 1)

    def send_acts(k):
        for d in range(1, J):
            remote(
                acts_block(k, plane_peer[d]), a_buf.at[rows(j * B, B), pl.ds(k * B, B)],
                acts_s.at[k], acts_r.at[k], in_plane[d],
            ).start()

    half = C // 2
    z_piece = j + 1 - 2 * lax.rem(j, 2)
    z_partner = {"fsdp": y * J + z_piece}
    along_x = (2, 4, 6)

    def cots_piece(owner, cols):
        return c_buf.at[rows(owner * B, B), cols]

    every, low_cols, high_cols = pl.ds(0, C), pl.ds(0, half), pl.ds(half, half)
    own_piece = cots_piece(j, every)
    remote(cots, own_piece, cots_s.at[0], cots_r.at[0], z_partner).start()
    for d in along_x:
        remote(cots, own_piece, cots_s.at[1], cots_r.at[1], in_plane[d]).start()
    for k in range(EARLY):
        send_acts(k)
    three = pl.ds(0, len(along_x) * B)
    cots_groups = [
        remote(c_buf.at[r, c], c_buf.at[r, c], cots_s.at[i], cots_r.at[i], z_partner)
        for i, (r, c) in enumerate(
            ((pl.ds(0, B), every), (three, every), (three, low_cols), (three, high_cols))
        )
    ]
    cots_groups[0].wait_recv()
    for d in along_x:
        piece = cots_piece(z_piece, high_cols)
        remote(piece, piece, cots_s.at[3], cots_r.at[3], in_plane[d]).start()
    cots_groups[1].wait_recv()
    for d in along_x:
        piece = cots_piece(plane_peer[d], low_cols)
        remote(piece, piece, cots_s.at[2], cots_r.at[2], z_partner).start()
    for k in range(EARLY, Y):
        send_acts(k)

    others = pl.ds(0, (J - 1) * B)

    def acts_arrivals(k):
        block = a_buf.at[others, pl.ds(k * B, B)]
        return remote(block, block, acts_s.at[k], acts_r.at[k], in_plane[1])

    own_cots.wait()
    cots_groups[2].wait_recv()
    cots_groups[3].wait_recv()

    def partial_gradient(k):
        own_acts[k].wait()
        acts_arrivals(k).wait_recv()
        return lax.dot_general(
            a_buf[:, pl.ds(k * B, B)], c_buf[...], (((0,), (0,)), ((), ())), preferred_element_type=F32
        )

    chain_cols = [pl.ds(s * (C // CHAIN), C // CHAIN) for s in range(CHAIN)]

    def chain(send_buf, recv_buf, send_sem, recv_sem, device):
        return [
            [
                remote(send_buf.at[i, :, cols], recv_buf.at[i, :, cols], send_sem.at[i, s], recv_sem.at[i, s], device)
                for s, cols in enumerate(chain_cols)
            ]
            for i in range(4)
        ]

    ups = chain(go_up, from_down, up_s, up_r, along_y[1])
    downs = chain(go_down, from_up, down_s, down_r, along_y[Y - 1])
    ups_first, downs_first = range(CHAIN // 2), range(CHAIN // 2, CHAIN)

    def add_and_send(i, part, copies, first_slices, send_buf, recv_buf):
        for s in range(CHAIN) if i else first_slices:
            cols = chain_cols[s]
            piece = part[:, s * (C // CHAIN) : (s + 1) * (C // CHAIN)]
            if i > 1 or i == 1 and s in first_slices:
                copies[i - 1][s].wait_recv()
                piece = piece + recv_buf[i - 1, :, cols].astype(F32)
            send_buf[i, :, cols] = piece.astype(BF16)
            copies[i][s].start()

    part = partial_gradient(SLOT[4])
    add_and_send(0, part, ups, ups_first, go_up, from_down)
    add_and_send(0, part, downs, downs_first, go_down, from_up)
    for i in range(1, 4):
        add_and_send(i, partial_gradient(SLOT[4 - i]), ups, ups_first, go_up, from_down)
        add_and_send(i, partial_gradient(SLOT[4 + i]), downs, downs_first, go_down, from_up)
    own_acts[OWN].wait()
    acts_arrivals(OWN).wait_recv()
    own_block = a_buf[:, pl.ds(OWN * B, B)].T
    for load in loads:
        load.wait()

    H = B // 2
    W = C // SLICES
    slices = [pl.ds(s * W, W) for s in range(SLICES)]

    def inner_step(s):
        cols = slices[s]
        if s * CHAIN % SLICES == 0:
            ups[3][s * CHAIN // SLICES].wait_recv()
            downs[3][s * CHAIN // SLICES].wait_recv()
        part = jnp.dot(own_block, c_buf[:, cols], preferred_element_type=F32)
        gradient = part + from_down[3, :, cols].astype(F32) + from_up[3, :, cols].astype(F32)
        first_next = decay_first * state[1, :, cols] + (1.0 - decay_first) * gradient
        first_buf[:, cols] = first_next
        second_next = decay_second * state[2, :, cols] + (1.0 - decay_second) * gradient * gradient
        stepped = state[0, :, cols] - inner_rate * first_next / (jnp.sqrt(second_next) + epsilon)
        stepped_buf[:, cols] = stepped
        pairs[s].start()

    pairs = [
        remote(stepped_buf.at[rows((1 - core) * H, H), cols], stepped_pair.at[:, cols], pair_s.at[s], pair_r.at[s], sibling)
        for s, cols in enumerate(slices)
    ]

    def z_copies(s):
        here = z_buf.at[zh, :, slices[s]]
        return [remote(here, here, z_s.at[s, q], z_r.at[s, q], along_z[q]) for q in range(1, Z)]

    zs = [z_copies(s) for s in range(SLICES)]

    def sum_cores(s):
        cols = slices[s]
        pairs[s].wait_recv()
        z_buf[zh, :, cols] = (stepped_buf[rows(core * H, H), cols] + stepped_pair[:, cols]).astype(BF16)
        for copy in zs[s]:
            copy.start()

    def w_half(s, t, side):
        return w_buf.at[SLOT[(Y - t) % Y], rows(side * H, H), slices[s]]

    def w_group(s, t, side):
        if t in (0, 4):
            return w_half(s, t, side)
        return w_buf.at[pl.ds(SLOT[t], 2), rows(side * H, H), slices[s]]

    near_first = (4, 3, 5, 2, 6, 1, 7)
    wys = [
        {t: remote(w_half(s, 0, core), w_half(s, t, core), wy_s.at[s, t], wy_r.at[s, t], along_y[t]) for t in near_first}
        for s in range(SLICES)
    ]
    forwards = [
        [remote(w_group(s, t, core), w_group(s, t, core), wc_s.at[s, t], wc_r.at[s, t], sibling) for t in range(5)]
        for s in range(SLICES)
    ]

    def outer_step(s):
        cols = slices[s]
        for q in range(1, Z):
            there = z_buf.at[lax.rem(zh + Z - q, Z), :, cols]
            remote(there, there, z_s.at[s, q], z_r.at[s, q], along_z[q]).wait_recv()
        sums = [z_buf[q, :, cols].astype(F32) for q in range(Z)]
        total = sums[0] + sums[1] + sums[2] + sums[3]
        mine = rows(core * H, H)
        average = state[3, mine, cols] - total / (2 * Z)
        velocity = outer_decay * state[4, mine, cols] + average
        weights = state[3, mine, cols] - outer_rate * (average + outer_decay * velocity)
        w_buf[OWN, rows(core * H, H), cols] = weights.astype(BF16)
        for t in near_first:
            wys[s][t].start()
        forwards[s][0].start()

    def to_sibling(s):
        for t in range(1, 5):
            wys[s][t].wait_recv()
            if t < 4:
                wys[s][Y - t].wait_recv()
            forwards[s][t].start()

    def values_of(s, d):
        return jnp.dot(a_buf[rows(plane_peer[d] * B, B), :], w_buf[:, :, slices[s]].reshape(Y * B, W), preferred_element_type=F32)

    vs = [
        [remote(v_send.at[s, d], v_recv.at[s, d], v_s.at[s, d], v_r.at[s, d], in_plane[d]) for d in range(1, J)]
        for s in range(SLICES)
    ]

    def send_values(s):
        for t in range(5):
            there = w_group(s, t, 1 - core)
            remote(there, there, wc_s.at[s, t], wc_r.at[s, t], sibling).wait_recv()
        for d in (4, 3, 5, 2, 6, 1, 7):
            v_send[s, d] = values_of(s, d).astype(BF16)
            vs[s][d - 1].start()

    stores = [
        pltpu.make_async_copy(v_out.at[:, cols], values_out.at[:, cols], values_sem.at[s]) for s, cols in enumerate(slices)
    ]

    def sum_values(s):
        total = values_of(s, 0)
        for d in range(1, J):
            vs[s][d - 1].wait_recv()
            total = total + v_recv[s, d].astype(F32)
        v_out[:, slices[s]] = total.astype(BF16)
        stores[s].start()

    for s in range(SLICES):
        inner_step(s)
        sum_cores(s)
    store_first = pltpu.make_async_copy(first_buf, first_out, first_sem)
    store_first.start()
    for s in range(SLICES):
        outer_step(s)
    for s in range(SLICES):
        to_sibling(s)
        send_values(s)
    for s in range(SLICES):
        sum_values(s)

    for copies in cots_groups:
        copies.wait_send()
    for k in range(Y):
        acts_arrivals(k).wait_send()
    for copies, first_slices in ((ups, ups_first), (downs, downs_first)):
        for i in range(4):
            for s in range(CHAIN) if i else first_slices:
                copies[i][s].wait_send()
    for s in range(SLICES):
        for copy in [pairs[s]] + zs[s] + list(wys[s].values()) + forwards[s] + vs[s]:
            copy.wait_send()
    store_first.wait()
    for store in stores:
        store.wait()


def on_device(acts, value_cots, inner_weights, first_moment, second_moment, anchor, outer_momentum):
    dma = pltpu.SemaphoreType.DMA
    vmem = pltpu.VMEM
    first_next, values = pl.pallas_call(
        step_kernel,
        name="diloco_step",
        out_shape=(jax.ShapeDtypeStruct((B, C), F32), jax.ShapeDtypeStruct((B, C), BF16)),
        in_specs=[pl.BlockSpec(memory_space=pl.ANY)] * 7,
        out_specs=(pl.BlockSpec(memory_space=pl.ANY), pl.BlockSpec(memory_space=pl.ANY)),
        scratch_shapes=[
            vmem((J * B, Y * B), BF16),
            vmem((J * B, C), BF16),
            vmem((5, B, C), F32),
            vmem((B, C), F32),
            vmem((4, B, C), BF16),
            vmem((4, B, C), BF16),
            vmem((4, B, C), BF16),
            vmem((4, B, C), BF16),
            vmem((B, C), F32),
            vmem((B // 2, C), F32),
            vmem((Z, B // 2, C), BF16),
            vmem((Y, B, C), BF16),
            vmem((SLICES, J, B, C // SLICES), BF16),
            vmem((SLICES, J, B, C // SLICES), BF16),
            vmem((B, C), BF16),
            dma((5,)),
            dma(()), dma((4,)), dma((4,)),
            dma((Y,)), dma((Y,)), dma((Y,)),
            dma((4, CHAIN)), dma((4, CHAIN)), dma((4, CHAIN)), dma((4, CHAIN)),
            dma((SLICES,)), dma((SLICES,)),
            dma((SLICES, Z)), dma((SLICES, Z)),
            dma((SLICES, Y)), dma((SLICES, Y)),
            dma((SLICES, Y)), dma((SLICES, Y)),
            dma((SLICES, J)), dma((SLICES, J)),
            dma(()), dma((SLICES,)),
        ],
        compiler_params=pltpu.CompilerParams(
            collective_id=0, has_side_effects=True, vmem_limit_bytes=62 * 1024 * 1024
        ),
    )(acts[0], value_cots[0], inner_weights[0], first_moment[0], second_moment[0], anchor, outer_momentum)
    return first_next[None], values[None]


def solution(mesh):
    placed = (
        P("rep", "fsdp", None),
        P("rep", "fsdp", None),
        P("rep", "fsdp", None),
        P("rep", "fsdp", None),
        P("rep", "fsdp", None),
        P("fsdp", None),
        P("fsdp", None),
    )
    return jax.shard_map(
        on_device,
        mesh=mesh,
        in_specs=placed,
        out_specs=(P("rep", "fsdp", None), P("rep", "fsdp", None)),
        check_vma=False,
    )
```

```python
import jax
import jax.numpy as jnp
from jax import lax
from jax.experimental import pallas as pl
from jax.experimental.pallas import tpu as pltpu
from jax.sharding import PartitionSpec as P

decay_first = 0.9
decay_second = 0.95
inner_rate = 0.006
epsilon = 1e-08
outer_rate = 0.7
outer_decay = 0.9

MESH = pl.DeviceIdType.MESH
F32 = jnp.float32
BF16 = jnp.bfloat16

Y = 8
J = 8
Z = 4
B = 128
C = 512
OFFSETS = (4, 3, 5, 2, 6, 1, 7, 0)
SLOT = {off: k for k, off in enumerate(OFFSETS)}
OWN = SLOT[0]
EARLY = 1
CHAIN = 2
SLICES = 4


def step_kernel(
    acts, cots, inner, first, second, anchor, momentum, first_out, values_out,
    a_buf, c_buf, state, first_buf, go_up, go_down, from_down, from_up,
    stepped_buf, stepped_pair, z_buf, w_buf, v_send, v_recv, v_out,
    state_sem, cots_own, cots_s, cots_r, acts_own, acts_s, acts_r, up_s, up_r, down_s, down_r,
    pair_s, pair_r, z_s, z_r, wy_s, wy_r, wc_s, wc_r, v_s, v_r, first_sem, values_sem,
):
    f = lax.axis_index("fsdp")
    r = lax.axis_index("rep")
    y, j = lax.div(f, J), lax.rem(f, J)
    zh, core = lax.div(r, 2), lax.rem(r, 2)
    plane_peer = [lax.rem(j + d, J) for d in range(J)]
    in_plane = [{"fsdp": y * J + plane_peer[d]} for d in range(J)]
    along_y = [{"fsdp": lax.rem(y + t, Y) * J + j} for t in range(Y)]
    along_z = [{"rep": lax.rem(zh + q, Z) * 2 + core} for q in range(Z)]
    sibling = {"rep": zh * 2 + 1 - core}

    def remote(src, dst, send, recv, device):
        return pltpu.make_async_remote_copy(
            src_ref=src, dst_ref=dst, send_sem=send, recv_sem=recv, device_id=device, device_id_type=MESH
        )

    def rows(start, size):
        return pl.ds(pl.multiple_of(start, size), size)

    barrier = pltpu.get_barrier_semaphore()
    for device in in_plane[1:] + along_y[1:] + along_z[1:] + [sibling]:
        pl.semaphore_signal(barrier, inc=1, device_id=device, device_id_type=MESH)

    own_cots = pltpu.make_async_copy(cots, c_buf.at[rows(j * B, B)], cots_own)
    own_cots.start()

    def acts_block(k, target):
        return acts.at[:, rows((lax.rem(y + OFFSETS[k], Y) * J + target) * B, B)]

    own_acts = [
        pltpu.make_async_copy(acts_block(k, j), a_buf.at[rows(j * B, B), pl.ds(k * B, B)], acts_own.at[k])
        for k in range(Y)
    ]
    for copy in own_acts:
        copy.start()
    loads = [
        pltpu.make_async_copy(ref, state.at[i], state_sem.at[i])
        for i, ref in enumerate((inner, first, second, anchor, momentum))
    ]
    for load in loads:
        load.start()
    pl.semaphore_wait(barrier, J - 1 + Y - 1 + Z - 1 + 1)

    def send_acts(k):
        for d in range(1, J):
            remote(
                acts_block(k, plane_peer[d]), a_buf.at[rows(j * B, B), pl.ds(k * B, B)],
                acts_s.at[k], acts_r.at[k], in_plane[d],
            ).start()

    half = C // 2
    z_piece = j + 1 - 2 * lax.rem(j, 2)
    z_partner = {"fsdp": y * J + z_piece}
    along_x = (2, 4, 6)

    def cots_piece(owner, cols):
        return c_buf.at[rows(owner * B, B), cols]

    every, low_cols, high_cols = pl.ds(0, C), pl.ds(0, half), pl.ds(half, half)
    own_piece = cots_piece(j, every)
    remote(cots, own_piece, cots_s.at[0], cots_r.at[0], z_partner).start()
    for d in along_x:
        remote(cots, own_piece, cots_s.at[1], cots_r.at[1], in_plane[d]).start()
    for k in range(EARLY):
        send_acts(k)
    three = pl.ds(0, len(along_x) * B)
    cots_groups = [
        remote(c_buf.at[r, c], c_buf.at[r, c], cots_s.at[i], cots_r.at[i], z_partner)
        for i, (r, c) in enumerate(
            ((pl.ds(0, B), every), (three, every), (three, low_cols), (three, high_cols))
        )
    ]
    cots_groups[0].wait_recv()
    for d in along_x:
        piece = cots_piece(z_piece, high_cols)
        remote(piece, piece, cots_s.at[3], cots_r.at[3], in_plane[d]).start()
    cots_groups[1].wait_recv()
    for d in along_x:
        piece = cots_piece(plane_peer[d], low_cols)
        remote(piece, piece, cots_s.at[2], cots_r.at[2], z_partner).start()
    for k in range(EARLY, Y):
        send_acts(k)

    others = pl.ds(0, (J - 1) * B)

    def acts_arrivals(k):
        block = a_buf.at[others, pl.ds(k * B, B)]
        return remote(block, block, acts_s.at[k], acts_r.at[k], in_plane[1])

    own_cots.wait()
    cots_groups[2].wait_recv()
    cots_groups[3].wait_recv()

    def partial_gradient(k):
        own_acts[k].wait()
        acts_arrivals(k).wait_recv()
        return lax.dot_general(
            a_buf[:, pl.ds(k * B, B)], c_buf[...], (((0,), (0,)), ((), ())), preferred_element_type=F32
        )

    chain_cols = [pl.ds(s * (C // CHAIN), C // CHAIN) for s in range(CHAIN)]

    def chain(send_buf, recv_buf, send_sem, recv_sem, device):
        return [
            [
                remote(send_buf.at[i, :, cols], recv_buf.at[i, :, cols], send_sem.at[i, s], recv_sem.at[i, s], device)
                for s, cols in enumerate(chain_cols)
            ]
            for i in range(4)
        ]

    ups = chain(go_up, from_down, up_s, up_r, along_y[1])
    downs = chain(go_down, from_up, down_s, down_r, along_y[Y - 1])
    ups_first, downs_first = range(CHAIN // 2), range(CHAIN // 2, CHAIN)

    def add_and_send(i, part, copies, first_slices, send_buf, recv_buf):
        for s in range(CHAIN) if i else first_slices:
            cols = chain_cols[s]
            piece = part[:, s * (C // CHAIN) : (s + 1) * (C // CHAIN)]
            if i > 1 or i == 1 and s in first_slices:
                copies[i - 1][s].wait_recv()
                piece = piece + recv_buf[i - 1, :, cols].astype(F32)
            send_buf[i, :, cols] = piece.astype(BF16)
            copies[i][s].start()

    part = partial_gradient(SLOT[4])
    add_and_send(0, part, ups, ups_first, go_up, from_down)
    add_and_send(0, part, downs, downs_first, go_down, from_up)
    for i in range(1, 4):
        add_and_send(i, partial_gradient(SLOT[4 - i]), ups, ups_first, go_up, from_down)
        add_and_send(i, partial_gradient(SLOT[4 + i]), downs, downs_first, go_down, from_up)
    own_acts[OWN].wait()
    acts_arrivals(OWN).wait_recv()
    own_block = a_buf[:, pl.ds(OWN * B, B)].T
    for load in loads:
        load.wait()

    H = B // 2
    W = C // SLICES
    slices = [pl.ds(s * W, W) for s in range(SLICES)]

    def inner_step(s):
        cols = slices[s]
        if s * CHAIN % SLICES == 0:
            ups[3][s * CHAIN // SLICES].wait_recv()
            downs[3][s * CHAIN // SLICES].wait_recv()
        part = jnp.dot(own_block, c_buf[:, cols], preferred_element_type=F32)
        gradient = part + from_down[3, :, cols].astype(F32) + from_up[3, :, cols].astype(F32)
        first_next = decay_first * state[1, :, cols] + (1.0 - decay_first) * gradient
        first_buf[:, cols] = first_next
        second_next = decay_second * state[2, :, cols] + (1.0 - decay_second) * gradient * gradient
        stepped = state[0, :, cols] - inner_rate * first_next / (jnp.sqrt(second_next) + epsilon)
        stepped_buf[:, cols] = stepped
        pairs[s].start()

    pairs = [
        remote(stepped_buf.at[rows((1 - core) * H, H), cols], stepped_pair.at[:, cols], pair_s.at[s], pair_r.at[s], sibling)
        for s, cols in enumerate(slices)
    ]

    def z_copies(s):
        here = z_buf.at[zh, :, slices[s]]
        return [remote(here, here, z_s.at[s, q], z_r.at[s, q], along_z[q]) for q in range(1, Z)]

    zs = [z_copies(s) for s in range(SLICES)]

    def sum_cores(s):
        cols = slices[s]
        pairs[s].wait_recv()
        z_buf[zh, :, cols] = (stepped_buf[rows(core * H, H), cols] + stepped_pair[:, cols]).astype(BF16)
        for copy in zs[s]:
            copy.start()

    def w_half(s, t, side):
        return w_buf.at[SLOT[(Y - t) % Y], rows(side * H, H), slices[s]]

    def w_group(s, t, side):
        if t in (0, 4):
            return w_half(s, t, side)
        return w_buf.at[pl.ds(SLOT[t], 2), rows(side * H, H), slices[s]]

    near_first = (4, 3, 5, 2, 6, 1, 7)
    wys = [
        {t: remote(w_half(s, 0, core), w_half(s, t, core), wy_s.at[s, t], wy_r.at[s, t], along_y[t]) for t in near_first}
        for s in range(SLICES)
    ]
    forwards = [
        [remote(w_group(s, t, core), w_group(s, t, core), wc_s.at[s, t], wc_r.at[s, t], sibling) for t in range(5)]
        for s in range(SLICES)
    ]

    def outer_step(s):
        cols = slices[s]
        for q in range(1, Z):
            there = z_buf.at[lax.rem(zh + Z - q, Z), :, cols]
            remote(there, there, z_s.at[s, q], z_r.at[s, q], along_z[q]).wait_recv()
        sums = [z_buf[q, :, cols].astype(F32) for q in range(Z)]
        total = sums[0] + sums[1] + sums[2] + sums[3]
        mine = rows(core * H, H)
        average = state[3, mine, cols] - total / (2 * Z)
        velocity = outer_decay * state[4, mine, cols] + average
        weights = state[3, mine, cols] - outer_rate * (average + outer_decay * velocity)
        w_buf[OWN, rows(core * H, H), cols] = weights.astype(BF16)
        for t in near_first:
            wys[s][t].start()
        forwards[s][0].start()

    def to_sibling(s):
        for t in range(1, 5):
            wys[s][t].wait_recv()
            if t < 4:
                wys[s][Y - t].wait_recv()
            forwards[s][t].start()

    def values_of(s, d):
        return jnp.dot(a_buf[rows(plane_peer[d] * B, B), :], w_buf[:, :, slices[s]].reshape(Y * B, W), preferred_element_type=F32)

    vs = [
        [remote(v_send.at[s, d], v_recv.at[s, d], v_s.at[s, d], v_r.at[s, d], in_plane[d]) for d in range(1, J)]
        for s in range(SLICES)
    ]

    def send_values(s):
        for t in range(5):
            there = w_group(s, t, 1 - core)
            remote(there, there, wc_s.at[s, t], wc_r.at[s, t], sibling).wait_recv()
        for d in range(1, J):
            v_send[s, d] = values_of(s, d).astype(BF16)
            vs[s][d - 1].start()

    stores = [
        pltpu.make_async_copy(v_out.at[:, cols], values_out.at[:, cols], values_sem.at[s]) for s, cols in enumerate(slices)
    ]

    def sum_values(s):
        total = values_of(s, 0)
        for d in range(1, J):
            vs[s][d - 1].wait_recv()
            total = total + v_recv[s, d].astype(F32)
        v_out[:, slices[s]] = total.astype(BF16)
        stores[s].start()

    for s in range(SLICES):
        inner_step(s)
        sum_cores(s)
    store_first = pltpu.make_async_copy(first_buf, first_out, first_sem)
    store_first.start()
    for s in range(SLICES):
        outer_step(s)
    for s in range(SLICES):
        to_sibling(s)
        send_values(s)
    for s in range(SLICES):
        sum_values(s)

    for copies in cots_groups:
        copies.wait_send()
    for k in range(Y):
        acts_arrivals(k).wait_send()
    for copies, first_slices in ((ups, ups_first), (downs, downs_first)):
        for i in range(4):
            for s in range(CHAIN) if i else first_slices:
                copies[i][s].wait_send()
    for s in range(SLICES):
        for copy in [pairs[s]] + zs[s] + list(wys[s].values()) + forwards[s] + vs[s]:
            copy.wait_send()
    store_first.wait()
    for store in stores:
        store.wait()


def on_device(acts, value_cots, inner_weights, first_moment, second_moment, anchor, outer_momentum):
    dma = pltpu.SemaphoreType.DMA
    vmem = pltpu.VMEM
    first_next, values = pl.pallas_call(
        step_kernel,
        name="diloco_step",
        out_shape=(jax.ShapeDtypeStruct((B, C), F32), jax.ShapeDtypeStruct((B, C), BF16)),
        in_specs=[pl.BlockSpec(memory_space=pl.ANY)] * 7,
        out_specs=(pl.BlockSpec(memory_space=pl.ANY), pl.BlockSpec(memory_space=pl.ANY)),
        scratch_shapes=[
            vmem((J * B, Y * B), BF16),
            vmem((J * B, C), BF16),
            vmem((5, B, C), F32),
            vmem((B, C), F32),
            vmem((4, B, C), BF16),
            vmem((4, B, C), BF16),
            vmem((4, B, C), BF16),
            vmem((4, B, C), BF16),
            vmem((B, C), F32),
            vmem((B // 2, C), F32),
            vmem((Z, B // 2, C), BF16),
            vmem((Y, B, C), BF16),
            vmem((SLICES, J, B, C // SLICES), BF16),
            vmem((SLICES, J, B, C // SLICES), BF16),
            vmem((B, C), BF16),
            dma((5,)),
            dma(()), dma((4,)), dma((4,)),
            dma((Y,)), dma((Y,)), dma((Y,)),
            dma((4, CHAIN)), dma((4, CHAIN)), dma((4, CHAIN)), dma((4, CHAIN)),
            dma((SLICES,)), dma((SLICES,)),
            dma((SLICES, Z)), dma((SLICES, Z)),
            dma((SLICES, Y)), dma((SLICES, Y)),
            dma((SLICES, Y)), dma((SLICES, Y)),
            dma((SLICES, J)), dma((SLICES, J)),
            dma(()), dma((SLICES,)),
        ],
        compiler_params=pltpu.CompilerParams(
            collective_id=0, has_side_effects=True, vmem_limit_bytes=62 * 1024 * 1024
        ),
    )(acts[0], value_cots[0], inner_weights[0], first_moment[0], second_moment[0], anchor, outer_momentum)
    return first_next[None], values[None]


def solution(mesh):
    placed = (
        P("rep", "fsdp", None),
        P("rep", "fsdp", None),
        P("rep", "fsdp", None),
        P("rep", "fsdp", None),
        P("rep", "fsdp", None),
        P("fsdp", None),
        P("fsdp", None),
    )
    return jax.shard_map(
        on_device,
        mesh=mesh,
        in_specs=placed,
        out_specs=(P("rep", "fsdp", None), P("rep", "fsdp", None)),
        check_vma=False,
    )
```
